512 devices in a mesh: bins: 32 (over z, x), xy: 16 (over y, core).
Axes of the slice: x: 4, y: 8, z: 8, core: 2. Of those that a mesh axis runs over, the one named last changes fastest.
Arguments:
- conc: float32 [32, 128, 64, 256], P('bins', None, 'xy'), may hold values from 0.05 to 2
- vel_x: float32 [32, 64, 256], P('bins', 'xy'), may hold values from -0.3 to 0.3
- vel_y: float32 [32, 64, 256], P('bins', 'xy'), may hold values from -0.3 to 0.3
- sea_mask: int32 [64, 256], P('xy'), may hold values 0 or 1
- settle: float32 [128], replicated, may hold values from 0.05 to 0.6
- size_bin_kernel_class: int32 [128], replicated, may hold values from 0 to 7
- aggregate_upward_factor: float32 [8], replicated, may hold values from 0.25 to 2
- agg_down: float32 [8], replicated, may hold values from 0.25 to 2
- break_rate: float32 [8], replicated, may hold values from 0.05 to 0.5
Outputs:
- conc_next: float32 [32, 128, 64, 256], P('bins', None, 'xy')
The draws below stay inside these ranges and needn't reach their ends.
All inputs are finite; a program needn't handle non-finite values. No bound on the sum of `sea_mask` on one device may be relied on, other than what follows from the above.
Results may differ from the reference program's by a relative error of at most 0.00007.
Values sent between devices are 32-bit elements; how exact they have to be, the bound alone decides.
A program may use at most 64 MiB of HBM per device.

```python
import math
import jax
import jax.numpy as jnp
from jax import lax

NB = 128
NCLS = 8
GY = 256
HSUB = 2
VERTICAL_SUBSTEP = 2
LEV = 32
GX = 64


def with_ends(array, own_key, low, top_value):
    place = [jax.random.randint(jax.random.fold_in(own_key, axis), (), 0, length) for axis, length in enumerate(array.shape)]
    longest = array.shape.index(max(array.shape))
    neighbour = place[:longest] + [(place[longest] + 1) % array.shape[longest]] + place[longest + 1:]
    return array.at[tuple(place)].set(low).at[tuple(neighbour)].set(top_value)


def levels(own_key, shape, cuts, smallest, largest):
    def one(dim, parts):
        heights = jax.random.uniform(jax.random.fold_in(jax.random.fold_in(own_key, 6), dim), (parts,), jnp.float32, smallest / len(cuts), largest / len(cuts))
        return jnp.repeat(jnp.exp(heights), shape[dim] // parts).reshape((-1,) + (1,) * (len(shape) - dim - 1))

    level = one(*cuts[0])
    for cut in cuts[1:]:
        level = level * one(*cut)
    return level


def setup_inputs(seed: int = 0) -> dict:
    splits = jax.random.split(jax.random.key(seed), 10)
    conc = jnp.clip(jnp.exp(math.log(2.0) - 3.6888794 * jax.random.uniform(splits[0], (LEV, NB, GX, GY), jnp.float32) ** levels(splits[0], (LEV, NB, GX, GY), ((0, 32), (2, 16)), -0.2, 0.2)), 0.05, 2.0)
    vel_x = jnp.clip(jax.random.uniform(splits[1], (LEV, GX, GY), jnp.float32, -0.3, 0.3) * levels(splits[1], (LEV, GX, GY), ((0, 32), (1, 16)), -0.4, 0.0), -0.3, 0.3)
    vel_y = jnp.clip(jax.random.uniform(splits[2], (LEV, GX, GY), jnp.float32, -0.3, 0.3) * levels(splits[2], (LEV, GX, GY), ((0, 32), (1, 16)), -0.4, 0.0), -0.3, 0.3)
    sea_mask = with_ends((jax.random.randint(splits[3], (GX, GY), 0, 4) < 3).astype(jnp.int32), jax.random.fold_in(splits[3], 1), 0, 1)
    settle = jnp.clip(jnp.exp(jax.random.uniform(splits[4], (NB,), jnp.float32, math.log(0.05), math.log(0.6))), 0.05, 0.6)
    size_bin_kernel_class = with_ends(jax.random.randint(splits[5], (NB,), 0, NCLS), jax.random.fold_in(splits[5], 1), 0, NCLS - 1).astype(jnp.int32)
    aggregate_upward_factor = jnp.clip(jnp.exp(jax.random.uniform(splits[6], (NCLS,), jnp.float32, math.log(0.25), math.log(2.0))), 0.25, 2.0)
    agg_down = jnp.clip(jnp.exp(jax.random.uniform(splits[7], (NCLS,), jnp.float32, math.log(0.25), math.log(2.0))), 0.25, 2.0)
    break_rate = jnp.clip(jnp.exp(jax.random.uniform(splits[8], (NCLS,), jnp.float32, math.log(0.05), math.log(0.5))), 0.05, 0.5)
    return {"conc": conc, "vel_x": vel_x, "vel_y": vel_y, "sea_mask": sea_mask, "settle": settle, "size_bin_kernel_class": size_bin_kernel_class, "aggregate_upward_factor": aggregate_upward_factor, "agg_down": agg_down, "break_rate": break_rate}


h_diffusion = 0.2
v_diffusion = 0.2
step_duration = 0.5
collide_scale = 2.0


def settle_mix(column, sink):
    flux = sink * column
    above = jnp.concatenate([jnp.zeros_like(flux[:1]), flux[:-1]], 0)
    upper = jnp.concatenate([column[:1], column[:-1]], 0)
    lower = jnp.concatenate([column[1:], column[-1:]], 0)
    return column - flux + above + v_diffusion * (upper + lower - 2.0 * column)


def reference(conc, vel_x, vel_y, sea_mask, settle, size_bin_kernel_class, aggregate_upward_factor, agg_down, break_rate):
    water = sea_mask.astype(jnp.float32)

    def horizontal(packed):
        level, speed_x, speed_y = packed
        for unused_item in range(HSUB):
            padded = jnp.pad(level, ((0, 0), (1, 1), (1, 1)))
            east = padded[:, 2:, 1:-1]
            west = padded[:, :-2, 1:-1]
            north = padded[:, 1:-1, 2:]
            south = padded[:, 1:-1, :-2]
            level = water * (level - 0.5 * speed_x * (east - west) - 0.5 * speed_y * (north - south)
                             + h_diffusion * (east + west + north + south - 4.0 * level))
        return level

    moved = lax.map(horizontal, (conc, vel_x, vel_y))
    sink = settle[:, None]
    up_rate = aggregate_upward_factor[size_bin_kernel_class][:, None]
    down_rate = agg_down[size_bin_kernel_class][:, None]
    brk_rate = break_rate[size_bin_kernel_class][:, None]
    bin_index = jnp.arange(NB)
    weight = (1.0 / jnp.maximum(bin_index, 1).astype(jnp.float32))[:, None]
    broken = (bin_index >= 1).astype(jnp.float32)[:, None]

    def column_row(block):
        for unused_item in range(VERTICAL_SUBSTEP):
            block = settle_mix(block, sink)
        up_terms = up_rate * block
        lower_sum = jnp.cumsum(up_terms, 1) - up_terms
        down_terms = down_rate * block
        higher_sum = jnp.sum(down_terms, 1, keepdims=True) - jnp.cumsum(down_terms, 1)
        fragmentation_terms = brk_rate * block * weight
        frag_sum = jnp.sum(fragmentation_terms, 1, keepdims=True) - jnp.cumsum(fragmentation_terms, 1)
        concentration_change = (collide_scale / NB) * (down_rate * block * lower_sum - up_rate * block * higher_sum)
        return block + step_duration * (concentration_change + frag_sum - brk_rate * broken * block)

    rows = jnp.moveaxis(moved, 2, 0)
    result = lax.map(column_row, rows)
    return jnp.moveaxis(result, 0, 2)
```

```python
import jax
import jax.numpy as jnp
from jax import lax
from jax.sharding import PartitionSpec as P

NB = 128
NCLS = 8
HSUB = 2
VERTICAL_SUBSTEP = 2


h_diffusion = 0.2
v_diffusion = 0.2
step_duration = 0.5
collide_scale = 2.0


def extended(cells, sides, width):
    for axis, dim in sides:
        count = lax.axis_size(axis)
        ends = count - 1
        head = lax.slice_in_dim(cells, 0, width, axis=dim)
        tail = lax.slice_in_dim(cells, cells.shape[dim] - width, cells.shape[dim], axis=dim)
        cells = jnp.concatenate(
            [
                lax.ppermute(tail, axis, [(i, (i + 1) % count) for i in range(ends)]),
                cells,
                lax.ppermute(head, axis, [((i + 1) % count, i) for i in range(ends)]),
            ],
            axis=dim,
        )
    return cells


def settle_mix(column, sink):
    flux = sink * column
    above = jnp.concatenate([jnp.zeros_like(flux[:1]), flux[:-1]], 0)
    upper = jnp.concatenate([column[:1], column[:-1]], 0)
    lower = jnp.concatenate([column[1:], column[-1:]], 0)
    return column - flux + above + v_diffusion * (upper + lower - 2.0 * column)


def local(
    conc,
    vel_x,
    vel_y,
    sea_mask,
    settle,
    size_bin_kernel_class,
    aggregate_upward_factor,
    agg_down,
    break_rate,
):
    water = sea_mask.astype(jnp.float32)
    speed_x = vel_x[:, None]
    speed_y = vel_y[:, None]
    level = conc
    for unused_item in range(HSUB):
        padded = extended(level, (("xy", 2),), 1)
        east = padded[:, :, 2:, :]
        west = padded[:, :, :-2, :]
        side = jnp.pad(level, ((0, 0), (0, 0), (0, 0), (1, 1)))
        north = side[:, :, :, 2:]
        south = side[:, :, :, :-2]
        level = water * (
            level
            - 0.5 * speed_x * (east - west)
            - 0.5 * speed_y * (north - south)
            + h_diffusion * (east + west + north + south - 4.0 * level)
        )
    count_bins = lax.axis_size("bins")
    local_size_bins = NB // count_bins
    first_bin = lax.axis_index("bins") * local_size_bins
    sink = lax.dynamic_slice_in_dim(settle, first_bin, local_size_bins)[:, None, None]
    block = lax.all_to_all(level, "bins", split_axis=1, concat_axis=0, tiled=True)
    for unused_item in range(VERTICAL_SUBSTEP):
        block = settle_mix(block, sink)
    block = lax.all_to_all(block, "bins", split_axis=0, concat_axis=1, tiled=True)[0]
    onehot = (size_bin_kernel_class[:, None] == jnp.arange(NCLS)[None, :]).astype(jnp.float32)
    up, down, brk = (
        jnp.dot(onehot, table, precision=lax.Precision.HIGHEST)
        for table in (aggregate_upward_factor, agg_down, break_rate)
    )
    bins = jnp.arange(NB)
    weight = 1.0 / jnp.maximum(bins, 1).astype(jnp.float32)
    broken = (bins >= 1).astype(jnp.float32)
    lower = (bins[None, :] < bins[:, None]).astype(jnp.float32)
    higher = (bins[None, :] > bins[:, None]).astype(jnp.float32)
    scale = collide_scale / NB
    flat = block.reshape(NB, -1)
    sums = jnp.dot(
        jnp.concatenate([lower * up[None, :], higher * down[None, :], higher * (brk * weight)[None, :]], 0),
        flat,
        precision=lax.Precision.HIGHEST,
    ).reshape((3,) + block.shape)
    up, down, brk = (part[:, None, None] for part in (up, down, brk * broken))
    result = block + step_duration * (
        scale * (down * block * sums[0] - up * block * sums[1]) + sums[2] - brk * block
    )
    return result[None]


def solution(mesh):
    placed = (
        P("bins", None, "xy", None),
        P("bins", "xy", None),
        P("bins", "xy", None),
        P("xy", None),
        P(),
        P(),
        P(),
        P(),
        P(),
    )
    return jax.shard_map(
        local, mesh=mesh, in_specs=placed, out_specs=P("bins", None, "xy", None), check_vma=False
    )
```

```python
import functools

import jax
import jax.numpy as jnp
from jax import lax
from jax.experimental import pallas as pl
from jax.experimental.pallas import tpu as pltpu
from jax.sharding import PartitionSpec as P

NB = 128
NCLS = 8

h_diffusion = 0.2
v_diffusion = 0.2
step_duration = 0.5
collide_scale = 2.0

MESH = pl.DeviceIdType.MESH
SUB, LANE = 8, 128
RING = 4
GROUP = NB // RING
PIECES = 4
PART = GROUP // PIECES
PAIRS = PART // 2
OFFSETS = (2, 1, 3, 0)
AUX = 2
MESSAGE = AUX + RING * PAIRS


def turn(value, shift, axis):
    return pltpu.roll(value, shift % value.shape[axis], axis)


def step_kernel(
    depth,
    bands,
    conc,
    vel_x,
    vel_y,
    sea_mask,
    settle,
    classes,
    up_table,
    down_table,
    break_table,
    out,
    up_out,
    down_out,
    up_in,
    down_in,
    moved,
    column,
    mixed,
    settled,
    rates,
    up_send,
    up_recv,
    down_send,
    down_recv,
    ring_send,
    ring_recv,
    deep_send,
    deep_recv,
    back_send,
    back_recv,
):
    place = lax.axis_index("bins")
    band = lax.axis_index("xy")
    z, x = place // RING, place % RING
    before, after = (band + bands - 1) % bands, (band + 1) % bands
    above, below = (z + depth - 1) % depth, (z + 1) % depth
    peers = [(place, before), (place, after), (above * RING + x, band), (below * RING + x, band)]
    peers += [(z * RING + (x + d) % RING, band) for d in (1, 2, 3)]
    barrier = pltpu.get_barrier_semaphore()
    for peer in peers:
        pl.semaphore_signal(barrier, inc=1, device_id=peer, device_id_type=MESH)

    sub = lax.broadcasted_iota(jnp.int32, (SUB, LANE), 0)
    lane = lax.broadcasted_iota(jnp.int32, (SUB, LANE), 1)
    row = sub % 4
    low = row < 2
    row_first, row_last = row == 0, row == 3
    lane_first, lane_last = lane == 0, lane == LANE - 1
    half = sub < 4
    main_seam = (half & lane_first) | (~half & lane_last)
    side_seam = (~half & lane_first) | (half & lane_last)
    keep_up = (band > 0).astype(jnp.float32)
    keep_down = (band < bands - 1).astype(jnp.float32)

    def pack(first, second):
        return (
            jnp.where(low, turn(first, 4, 0), turn(second, 6, 0)) * keep_up,
            jnp.where(low, turn(first, 2, 0), turn(second, 4, 0)) * keep_down,
        )

    def unpack(upper, lower):
        return (
            jnp.where(low, upper, turn(lower, 2, 0)),
            jnp.where(low, turn(upper, 6, 0), lower),
        )

    def plane(ref):
        whole = ref[...].reshape(4, 2 * LANE)
        return jnp.concatenate([whole[:, :LANE], whole[:, LANE:]], 0)

    water = plane(sea_mask).astype(jnp.float32)
    speed_x, speed_y = plane(vel_x), plane(vel_y)
    for spot, pair in enumerate(((speed_x, speed_y), (water, water))):
        upper, lower = pack(*pair)
        up_out[0, spot] = upper
        down_out[0, spot] = lower

    def fill(j, unused):
        for n, d in enumerate(OFFSETS):
            first = (x + d) % RING * GROUP + j * PART
            for t in range(PAIRS):
                upper, lower = pack(conc[first + 2 * t], conc[first + 2 * t + 1])
                up_out[j, AUX + n * PAIRS + t] = upper
                down_out[j, AUX + n * PAIRS + t] = lower
        return unused

    lax.fori_loop(0, PIECES, fill, 0)
    pl.semaphore_wait(barrier, len(peers))

    def halo(j, start):
        rows = pl.ds(start, MESSAGE - start)
        return (
            pltpu.make_async_remote_copy(
                src_ref=up_out.at[j, rows],
                dst_ref=up_in.at[j, rows],
                send_sem=up_send.at[j],
                recv_sem=up_recv.at[j],
                device_id=(place, before),
                device_id_type=MESH,
            ),
            pltpu.make_async_remote_copy(
                src_ref=down_out.at[j, rows],
                dst_ref=down_in.at[j, rows],
                send_sem=down_send.at[j],
                recv_sem=down_recv.at[j],
                device_id=(place, after),
                device_id_type=MESH,
            ),
        )

    def ring(j, d):
        return pltpu.make_async_remote_copy(
            src_ref=moved.at[d, pl.ds(j * PART, PART)],
            dst_ref=column.at[2 + x, pl.ds(j * PART, PART)],
            send_sem=ring_send.at[j, d],
            recv_sem=ring_recv.at[j, d],
            device_id=(z * RING + (x + d) % RING, band),
            device_id_type=MESH,
        )

    def deep(j):
        part = pl.ds(j * PART, PART)
        return (
            pltpu.make_async_remote_copy(
                src_ref=column.at[pl.ds(4, 2), part],
                dst_ref=column.at[pl.ds(0, 2), part],
                send_sem=deep_send.at[j, 0],
                recv_sem=deep_recv.at[j, 0],
                device_id=(below * RING + x, band),
                device_id_type=MESH,
            ),
            pltpu.make_async_remote_copy(
                src_ref=column.at[pl.ds(2, 2), part],
                dst_ref=column.at[pl.ds(6, 2), part],
                send_sem=deep_send.at[j, 1],
                recv_sem=deep_recv.at[j, 1],
                device_id=(above * RING + x, band),
                device_id_type=MESH,
            ),
        )

    def back(j, d):
        part = pl.ds(j * PART, PART)
        return pltpu.make_async_remote_copy(
            src_ref=mixed.at[(x + d) % RING, part],
            dst_ref=settled.at[x, part],
            send_sem=back_send.at[j, d],
            recv_sem=back_recv.at[j, d],
            device_id=(z * RING + (x + d) % RING, band),
            device_id_type=MESH,
        )

    for j in range(PIECES):
        for copy in halo(j, 0 if j == 0 else AUX):
            copy.start()

    def rate(b, unused):
        own = classes[b]
        bin_index = jnp.maximum(b, 1).astype(jnp.float32)
        r = step_duration * break_table[own]
        rates[0, b] = up_table[own]
        rates[1, b] = down_table[own]
        rates[2, b] = r / bin_index
        rates[3, b] = 1.0 - r * jnp.minimum(b, 1).astype(jnp.float32)
        return unused

    lax.fori_loop(0, NB, rate, 0)

    def weights(mask, along, across):
        return (
            (1.0 - 4.0 * h_diffusion) * mask,
            mask * (h_diffusion - 0.5 * along),
            mask * (h_diffusion + 0.5 * along),
            mask * (h_diffusion - 0.5 * across),
            mask * (h_diffusion + 0.5 * across),
        )

    def transport(cells, rest, seam, factors):
        own, east_f, west_f, north_f, south_f = factors
        east = turn(jnp.where(row_first, rest, cells), -1, 0)
        west = turn(jnp.where(row_last, rest, cells), 1, 0)
        swapped = jnp.where(seam, turn(cells, 4, 0), 0.0)
        north = turn(jnp.where(lane_first, swapped, cells), -1, 1)
        south = turn(jnp.where(lane_last, swapped, cells), 1, 1)
        return own * cells + east_f * east + west_f * west + north_f * north + south_f * south

    main = weights(water, speed_x, speed_y)
    for copy in halo(0, 0):
        copy.wait_recv()
    side_x, side_y = unpack(up_in[0, 0], down_in[0, 0])
    side_water, _ = unpack(up_in[0, 1], down_in[0, 1])
    side = weights(side_water, side_x, side_y)

    def horizontal(j, unused):
        @pl.when(j > 0)
        def _():
            for copy in halo(j, AUX):
                copy.wait_recv()

        for n, d in enumerate(OFFSETS):
            first = (x + d) % RING * GROUP + j * PART
            for t in range(PAIRS):
                spot = AUX + n * PAIRS + t
                rests = unpack(up_in[j, spot], down_in[j, spot])
                for i, rest in enumerate(rests):
                    cells = conc[first + 2 * t + i]
                    once = transport(cells, rest, main_seam, main)
                    rest = transport(rest, cells, side_seam, side)
                    twice = transport(once, rest, main_seam, main)
                    if d:
                        moved[d, j * PART + 2 * t + i] = twice
                    else:
                        column[2 + x, j * PART + 2 * t + i] = twice
            if d:
                ring(j, d).start()
        return unused

    lax.fori_loop(0, PIECES, horizontal, 0)

    def forward(j):
        for d in (1, 2, 3):
            ring(j, d).wait_recv()
        for copy in deep(j):
            copy.start()

    top, bottom = z == 0, z == depth - 1

    def settle_mix(levels, sink, start):
        share = v_diffusion
        keep, fall = 1.0 - 2.0 * share - sink, share + sink
        count = len(levels) - 2
        fresh = []
        for k in range(count):
            upper, own, lower = levels[k : k + 3]
            upper_term = fall * upper
            lower_term = share * lower
            if start + k == 2:
                upper_term = jnp.where(top, share * own, upper_term)
            if start + k == 5:
                lower_term = jnp.where(bottom, share * own, lower_term)
            fresh.append(keep * own + upper_term + lower_term)
        return fresh

    def vertical(j):
        for copy in deep(j):
            copy.wait_recv()
        for i in range(PART):
            spot = j * PART + i
            sink = settle[x * GROUP + spot]
            levels = [column[k, spot] for k in range(8)]
            levels = settle_mix(settle_mix(levels, sink, 1), sink, 2)
            for k in range(RING):
                mixed[k, spot] = levels[k]
            settled[x, spot] = mixed[x, spot]
        for d in (2, 1, 3):
            back(j, d).start()

    forward(0)

    def middle(j, unused):
        forward(j)
        vertical(j - 1)
        return unused

    lax.fori_loop(1, PIECES, middle, 0)
    vertical(PIECES - 1)

    def arrive(j, unused):
        for d in (1, 2, 3):
            back(j, d).wait_recv()
        return unused

    lax.fori_loop(0, PIECES, arrive, 0)

    zero = jnp.zeros((SUB, LANE), jnp.float32)

    def totals(b, sums):
        higher, pieces = sums
        cells = settled[b // GROUP, b % GROUP]
        return higher + rates[1, b] * cells, pieces + rates[2, b] * cells

    higher, pieces = lax.fori_loop(0, NB, totals, (zero, zero), unroll=8)

    def collide(b, sums):
        lower, higher, pieces = sums
        cells = settled[b // GROUP, b % GROUP]
        gain, loss = rates[1, b], rates[0, b]
        higher = higher - gain * cells
        pieces = pieces - rates[2, b] * cells
        change = (step_duration * collide_scale / NB) * (gain * lower - loss * higher)
        out[b] = cells * (rates[3, b] + change) + pieces
        return lower + loss * cells, higher, pieces

    lax.fori_loop(0, NB, collide, (zero, higher, pieces), unroll=8)

    for j in range(PIECES):
        for copy in halo(j, 0 if j == 0 else AUX):
            copy.wait_send()

    def drain(j, unused):
        for d in (1, 2, 3):
            ring(j, d).wait_send()
            back(j, d).wait_send()
        for copy in deep(j):
            copy.wait_send()
        return unused

    lax.fori_loop(0, PIECES, drain, 0)


def local(depth, bands, conc, *rest):
    cells = conc.reshape(NB, 4, 2, LANE).transpose(0, 2, 1, 3).reshape(NB, SUB, LANE)
    vmem = pl.BlockSpec(memory_space=pltpu.VMEM)
    smem = pl.BlockSpec(memory_space=pltpu.SMEM)
    dma = pltpu.SemaphoreType.DMA
    tile = (SUB, LANE)

    def buffer(*shape):
        return pltpu.VMEM(shape + tile, jnp.float32)

    result = pl.pallas_call(
        functools.partial(step_kernel, depth, bands),
        out_shape=jax.ShapeDtypeStruct((NB,) + tile, jnp.float32),
        in_specs=[vmem] * 4 + [smem] * 5,
        out_specs=vmem,
        scratch_shapes=[
            buffer(PIECES, MESSAGE),
            buffer(PIECES, MESSAGE),
            buffer(PIECES, MESSAGE),
            buffer(PIECES, MESSAGE),
            buffer(RING, GROUP),
            buffer(8, GROUP),
            buffer(RING, GROUP),
            buffer(RING, GROUP),
            pltpu.SMEM((4, NB), jnp.float32),
            dma((PIECES,)),
            dma((PIECES,)),
            dma((PIECES,)),
            dma((PIECES,)),
            dma((PIECES, RING)),
            dma((PIECES, RING)),
            dma((PIECES, 2)),
            dma((PIECES, 2)),
            dma((PIECES, RING)),
            dma((PIECES, RING)),
        ],
        compiler_params=pltpu.CompilerParams(collective_id=0, has_side_effects=True),
    )(cells, *rest)
    return result.reshape(NB, 2, 4, LANE).transpose(0, 2, 1, 3).reshape(conc.shape)


def solution(mesh):
    placed = (
        P("bins", None, "xy", None),
        P("bins", "xy", None),
        P("bins", "xy", None),
        P("xy", None),
        P(),
        P(),
        P(),
        P(),
        P(),
    )
    return jax.shard_map(
        functools.partial(local, mesh.shape["bins"] // RING, mesh.shape["xy"]),
        mesh=mesh,
        in_specs=placed,
        out_specs=P("bins", None, "xy", None),
        check_vma=False,
    )
```

```python
import functools

import jax
import jax.numpy as jnp
from jax import lax
from jax.experimental import pallas as pl
from jax.experimental.pallas import tpu as pltpu
from jax.sharding import PartitionSpec as P

NB = 128
NCLS = 8

h_diffusion = 0.2
v_diffusion = 0.2
step_duration = 0.5
collide_scale = 2.0

MESH = pl.DeviceIdType.MESH
SUB, LANE = 8, 128
RING = 4
GROUP = NB // RING
PIECES = 4
PART = GROUP // PIECES
QUADS = PART // 4
OFFSETS = (2, 1, 3, 0)
AUX = 3
MESSAGE = AUX + RING * QUADS * 2
ALPHA = step_duration * collide_scale / NB


def turn(value, shift, axis):
    return pltpu.roll(value, shift % value.shape[axis], axis)


def step_kernel(
    depth,
    bands,
    conc_hbm,
    vel_x_hbm,
    vel_y_hbm,
    sea_mask_hbm,
    settle_hbm,
    classes_hbm,
    up_hbm,
    down_hbm,
    break_hbm,
    settled,
    tables,
    conc,
    vel_x,
    vel_y,
    sea_mask,
    settle,
    classes,
    up_table,
    down_table,
    break_table,
    up_out,
    down_out,
    up_in,
    down_in,
    moved,
    column,
    mixed,
    sinks,
    factors,
    load_sem,
    enter_sem,
    up_send,
    up_recv,
    down_send,
    down_recv,
    ring_send,
    ring_recv,
    deep_send,
    deep_recv,
    back_send,
    back_recv,
):
    place = lax.axis_index("bins")
    band = lax.axis_index("xy")
    z, x = place // RING, place % RING
    top, bottom = z == 0, z == depth - 1
    first_band, last_band = band == 0, band == bands - 1
    barrier = pltpu.get_barrier_semaphore()

    def greet(bins, xy):
        pl.semaphore_signal(barrier, inc=1, device_id=(bins, xy), device_id_type=MESH)

    for d in (1, 2, 3):
        greet(z * RING + (x + d) % RING, band)
    pl.when(~first_band)(lambda: greet(place, band - 1))
    pl.when(~last_band)(lambda: greet(place, band + 1))
    pl.when(~bottom)(lambda: greet(place + RING, band))

    loads = [
        pltpu.make_async_copy(src, dst, load_sem.at[i])
        for i, (src, dst) in enumerate(
            (
                (conc_hbm, conc),
                (vel_x_hbm, vel_x),
                (vel_y_hbm, vel_y),
                (sea_mask_hbm, sea_mask),
                (settle_hbm, settle),
                (classes_hbm, classes),
                (up_hbm, up_table),
                (down_hbm, down_table),
                (break_hbm, break_table),
            )
        )
    ]
    for copy in loads:
        copy.start()

    zero = jnp.zeros((SUB, LANE), jnp.float32)

    @pl.when(first_band)
    def _():
        down_in[...] = jnp.zeros_like(down_in)

    @pl.when(last_band)
    def _():
        up_in[...] = jnp.zeros_like(up_in)

    sub = lax.broadcasted_iota(jnp.int32, (SUB, LANE), 0)
    lane = lax.broadcasted_iota(jnp.int32, (SUB, LANE), 1)
    even = sub % 2 == 0
    low = sub % 4 < 2
    lane_first, lane_last = lane == 0, lane == LANE - 1
    half = sub < 4
    seam = (half & lane_first) | (~half & lane_last)

    def swap_rows(a, b, c, d):
        ab, ba = jnp.where(even, a, turn(b, 1, 0)), jnp.where(even, turn(a, -1, 0), b)
        cd, dc = jnp.where(even, c, turn(d, 1, 0)), jnp.where(even, turn(c, -1, 0), d)
        return (
            jnp.where(low, ab, turn(cd, 2, 0)),
            jnp.where(low, ba, turn(dc, 2, 0)),
            jnp.where(low, turn(ab, -2, 0), cd),
            jnp.where(low, turn(ba, -2, 0), dc),
        )

    for copy in loads:
        copy.wait()

    def plane(ref):
        whole = ref[...].reshape(4, 2 * LANE)
        return jnp.concatenate([whole[:, :LANE], whole[:, LANE:]], 0)

    fields = [
        swap_rows(*[value] * 4)
        for value in (plane(vel_x), plane(vel_y), plane(sea_mask).astype(jnp.float32))
    ]
    for k, rows in enumerate(fields):
        up_out[0, k] = rows[0]
        down_out[0, k] = rows[3]

    def pack(j):
        for n, d in enumerate(OFFSETS):
            for q in range(QUADS):
                first = (x + d) % RING * GROUP + j * PART + 4 * q
                rows = swap_rows(*[conc[first + i] for i in range(4)])
                spot = AUX + (n * QUADS + q) * 2
                up_out[j, spot], up_out[j, spot + 1] = rows[0], rows[1]
                down_out[j, spot], down_out[j, spot + 1] = rows[2], rows[3]

    def halo_up(j, start):
        rows = pl.ds(start, MESSAGE - start)
        return pltpu.make_async_remote_copy(
            src_ref=up_out.at[j, rows],
            dst_ref=up_in.at[j, rows],
            send_sem=up_send.at[j],
            recv_sem=up_recv.at[j],
            device_id=(place, band - 1),
            device_id_type=MESH,
        )

    def halo_down(j, start):
        rows = pl.ds(start, MESSAGE - start)
        return pltpu.make_async_remote_copy(
            src_ref=down_out.at[j, rows],
            dst_ref=down_in.at[j, rows],
            send_sem=down_send.at[j],
            recv_sem=down_recv.at[j],
            device_id=(place, band + 1),
            device_id_type=MESH,
        )

    def ring(j, d):
        return pltpu.make_async_remote_copy(
            src_ref=moved.at[d, pl.ds(j * PART, PART)],
            dst_ref=column.at[2 + x, pl.ds(j * PART, PART)],
            send_sem=ring_send.at[j, d],
            recv_sem=ring_recv.at[j, d],
            device_id=(z * RING + (x + d) % RING, band),
            device_id_type=MESH,
        )

    def deep_down(j):
        part = pl.ds(j * PART, PART)
        return pltpu.make_async_remote_copy(
            src_ref=column.at[pl.ds(4, 2), part],
            dst_ref=column.at[pl.ds(0, 2), part],
            send_sem=deep_send.at[j, 0],
            recv_sem=deep_recv.at[j, 0],
            device_id=(place + RING, band),
            device_id_type=MESH,
        )

    def deep_up(j):
        part = pl.ds(j * PART, PART)
        return pltpu.make_async_remote_copy(
            src_ref=column.at[pl.ds(2, 2), part],
            dst_ref=column.at[pl.ds(6, 2), part],
            send_sem=deep_send.at[j, 1],
            recv_sem=deep_recv.at[j, 1],
            device_id=(place - RING, band),
            device_id_type=MESH,
        )

    def back(j, d):
        part = pl.ds(j * PART, PART)
        return pltpu.make_async_remote_copy(
            src_ref=mixed.at[(x + d) % RING, part],
            dst_ref=settled.at[x, part],
            send_sem=back_send.at[j, d],
            recv_sem=back_recv.at[j, d],
            device_id=(z * RING + (x + d) % RING, band),
            device_id_type=MESH,
        )

    def send_halo(j, start):
        pl.when(~first_band)(lambda: halo_up(j, start).start())
        pl.when(~last_band)(lambda: halo_down(j, start).start())

    def take_halo(j, start):
        pl.when(~last_band)(lambda: halo_up(j, start).wait_recv())
        pl.when(~first_band)(lambda: halo_down(j, start).wait_recv())

    pack(0)
    greeted = 3 + (1 - first_band.astype(jnp.int32)) + (1 - last_band.astype(jnp.int32))
    pl.semaphore_wait(barrier, greeted + (1 - top.astype(jnp.int32)))
    send_halo(0, 0)

    @pl.when(~top)
    def _():
        pl.semaphore_signal(
            enter_sem, inc=1, device_id=(place - RING, band), device_id_type=MESH
        )

    def rest_pack(j, unused):
        pack(j)
        send_halo(j, AUX)
        return unused

    lax.fori_loop(1, PIECES, rest_pack, 0)

    def spread(value):
        return jnp.broadcast_to(value.reshape(1, NB), (NB, NB)).T

    own_class = classes[...].reshape(1, NB)
    bins = lax.broadcasted_iota(jnp.int32, (1, NB), 1)

    def lookup(table):
        value = jnp.zeros((1, NB), jnp.float32)
        for k in range(NCLS):
            value = jnp.where(own_class == k, table[k], value)
        return value

    rate = step_duration * lookup(break_table)
    sinks[...] = spread(settle[...])
    tables[0] = spread(lookup(up_table))
    tables[1] = spread(lookup(down_table))
    tables[2] = spread(rate / jnp.maximum(bins, 1).astype(jnp.float32))
    tables[3] = spread(jnp.where(bins >= 1, 1.0 - rate, 1.0))

    def weights(spot, along, across, mask):
        factors[spot, 0] = (1.0 - 4.0 * h_diffusion) * mask
        factors[spot, 1] = mask * (h_diffusion - 0.5 * along)
        factors[spot, 2] = mask * (h_diffusion + 0.5 * along)
        factors[spot, 3] = mask * (h_diffusion - 0.5 * across)
        factors[spot, 4] = mask * (h_diffusion + 0.5 * across)

    for r in range(4):
        weights(1 + r, *[rows[r] for rows in fields])
    take_halo(0, 0)
    weights(0, *[down_in[0, k] for k in range(AUX)])
    weights(5, *[up_in[0, k] for k in range(AUX)])

    def transport(west, cells, east, spot):
        swapped = jnp.where(seam, turn(cells, 4, 0), 0.0)
        north = turn(jnp.where(lane_first, swapped, cells), -1, 1)
        south = turn(jnp.where(lane_last, swapped, cells), 1, 1)
        return (
            factors[spot, 0] * cells
            + factors[spot, 1] * east
            + factors[spot, 2] * west
            + factors[spot, 3] * north
            + factors[spot, 4] * south
        )

    def horizontal(j, unused):
        pl.when(j > 0)(lambda: take_halo(j, AUX))
        for n, d in enumerate(OFFSETS):
            for q in range(QUADS):
                spot = AUX + (n * QUADS + q) * 2
                rows = [
                    ref[j, spot + i] for ref in (down_in, up_out, down_out, up_in) for i in (0, 1)
                ]
                once = [transport(*rows[r : r + 3], r) for r in range(6)]
                for r in range(4):
                    twice = transport(*once[r : r + 3], 1 + r)
                    if d:
                        moved[d, j * PART + 4 * q + r] = twice
                    else:
                        column[2 + x, j * PART + 4 * q + r] = twice
            if d:
                ring(j, d).start()
        return unused

    lax.fori_loop(0, PIECES, horizontal, 0)
    pl.when(~bottom)(lambda: pl.semaphore_wait(enter_sem, 1))

    def forward(j):
        for d in (1, 2, 3):
            ring(j, d).wait_recv()
        pl.when(~top)(lambda: deep_up(j).start())
        pl.when(~bottom)(lambda: deep_down(j).start())

    def settle_mix(levels, sink, start):
        share = v_diffusion
        keep, fall = 1.0 - 2.0 * share - sink, share + sink
        fresh = []
        for k in range(len(levels) - 2):
            upper, own, lower = levels[k : k + 3]
            upper_term = fall * upper
            lower_term = share * lower
            if start + k == 2:
                upper_term = jnp.where(top, share * own, upper_term)
            if start + k == 5:
                lower_term = jnp.where(bottom, share * own, lower_term)
            fresh.append(keep * own + upper_term + lower_term)
        return fresh

    def vertical(j):
        pl.when(~top)(lambda: deep_down(j).wait_recv())
        pl.when(~bottom)(lambda: deep_up(j).wait_recv())
        sink = sinks[pl.ds(pl.multiple_of(x * GROUP + j * PART, PART), PART)]
        other = turn(sink, 4, 0)
        for q in range(QUADS):
            own_sink = jnp.where(half, sink, other) if q == 0 else jnp.where(half, other, sink)
            spot = j * PART + 4 * q
            rows = []
            for r in range(4):
                levels = [column[k, spot + r] for k in range(8)]
                rows.append(settle_mix(settle_mix(levels, own_sink, 1), own_sink, 2))
            for k in range(RING):
                for i, cells in enumerate(swap_rows(*[levels[k] for levels in rows])):
                    mixed[k, spot + i] = cells
        for d in (2, 1, 3):
            back(j, d).start()
        for i in range(PART):
            settled[x, j * PART + i] = mixed[x, j * PART + i]

    forward(0)

    def middle(j, unused):
        forward(j)
        vertical(j - 1)
        return unused

    lax.fori_loop(1, PIECES, middle, 0)
    vertical(PIECES - 1)

    def drain(j, unused):
        for d in (1, 2, 3):
            back(j, d).wait_recv()
            ring(j, d).wait_send()
            back(j, d).wait_send()
        pl.when(~top)(lambda: deep_up(j).wait_send())
        pl.when(~bottom)(lambda: deep_down(j).wait_send())
        return unused

    def drain_halo(j, start):
        pl.when(~first_band)(lambda: halo_up(j, start).wait_send())
        pl.when(~last_band)(lambda: halo_down(j, start).wait_send())

    lax.fori_loop(0, PIECES, drain, 0)
    for j in range(PIECES):
        drain_halo(j, 0 if j == 0 else AUX)


def collide_kernel(settled, tables, out, sums):
    parts = NB // PART

    def row(k, b):
        return jnp.broadcast_to(tables[k, pl.ds(b, 1)], (SUB, LANE))

    def total(p, unused):
        b = p * PART
        cells = [settled[b + i] for i in range(PART)]
        for k in range(3):
            terms = [row(k, b + i) * cells[i] for i in range(PART)]
            while len(terms) > 1:
                terms = [one + two for one, two in zip(terms[::2], terms[1::2])]
            sums[k, p] = terms[0]
        return unused

    lax.fori_loop(0, parts, total, 0, unroll=2)
    lower = jnp.zeros((SUB, LANE), jnp.float32)
    for p in range(parts):
        own = sums[0, p]
        sums[0, p] = lower
        lower = lower + own
    for k in (1, 2):
        higher = jnp.zeros((SUB, LANE), jnp.float32)
        for p in reversed(range(parts)):
            higher = higher + sums[k, p]
            sums[k, p] = higher

    def collide(p, unused):
        lower, higher, pieces = sums[0, p], sums[1, p], sums[2, p]
        for i in range(PART):
            b = p * PART + i
            cells = settled[b]
            loss, gain = row(0, b), row(1, b)
            higher = higher - gain * cells
            pieces = pieces - row(2, b) * cells
            out[b] = cells * (row(3, b) + ALPHA * (gain * lower - loss * higher)) + pieces
            lower = lower + loss * cells
        return unused

    lax.fori_loop(0, parts, collide, 0, unroll=2)


def local(depth, bands, conc, *rest):
    cells = conc.reshape(NB, 4, 2, LANE).transpose(0, 2, 1, 3).reshape(NB, SUB, LANE)
    vmem = pl.BlockSpec(memory_space=pltpu.VMEM)
    dma = pltpu.SemaphoreType.DMA
    tile = (SUB, LANE)

    def buffer(*shape):
        return pltpu.VMEM(shape + tile, jnp.float32)

    settled, tables = pl.pallas_call(
        functools.partial(step_kernel, depth, bands),
        out_shape=(
            jax.ShapeDtypeStruct((RING, GROUP) + tile, jnp.float32),
            jax.ShapeDtypeStruct((4, NB, LANE), jnp.float32),
        ),
        in_specs=[pl.BlockSpec(memory_space=pltpu.HBM)] * 9,
        out_specs=(vmem, vmem),
        scratch_shapes=[
            buffer(NB),
            pltpu.VMEM((1, 4, 2 * LANE), jnp.float32),
            pltpu.VMEM((1, 4, 2 * LANE), jnp.float32),
            pltpu.VMEM((4, 2 * LANE), jnp.int32),
            pltpu.VMEM((NB,), jnp.float32),
            pltpu.VMEM((NB,), jnp.int32),
            pltpu.SMEM((NCLS,), jnp.float32),
            pltpu.SMEM((NCLS,), jnp.float32),
            pltpu.SMEM((NCLS,), jnp.float32),
            buffer(PIECES, MESSAGE),
            buffer(PIECES, MESSAGE),
            buffer(PIECES, MESSAGE),
            buffer(PIECES, MESSAGE),
            buffer(RING, GROUP),
            buffer(8, GROUP),
            buffer(RING, GROUP),
            pltpu.VMEM((NB, LANE), jnp.float32),
            buffer(6, 5),
            dma((9,)),
            pltpu.SemaphoreType.REGULAR,
            dma((PIECES,)),
            dma((PIECES,)),
            dma((PIECES,)),
            dma((PIECES,)),
            dma((PIECES, RING)),
            dma((PIECES, RING)),
            dma((PIECES, 2)),
            dma((PIECES, 2)),
            dma((PIECES, RING)),
            dma((PIECES, RING)),
        ],
        compiler_params=pltpu.CompilerParams(
            collective_id=0, has_side_effects=True, vmem_limit_bytes=20 << 20
        ),
    )(cells, *rest)
    result = pl.pallas_call(
        collide_kernel,
        out_shape=jax.ShapeDtypeStruct((NB,) + tile, jnp.float32),
        in_specs=[vmem, vmem],
        out_specs=vmem,
        scratch_shapes=[buffer(3, NB // PART)],
        compiler_params=pltpu.CompilerParams(vmem_limit_bytes=8 << 20),
    )(settled.reshape((NB,) + tile), tables)
    return result.reshape(NB, 2, 4, LANE).transpose(0, 2, 1, 3).reshape(conc.shape)


def solution(mesh):
    placed = (
        P("bins", None, "xy", None),
        P("bins", "xy", None),
        P("bins", "xy", None),
        P("xy", None),
        P(),
        P(),
        P(),
        P(),
        P(),
    )
    return jax.shard_map(
        functools.partial(local, mesh.shape["bins"] // RING, mesh.shape["xy"]),
        mesh=mesh,
        in_specs=placed,
        out_specs=P("bins", None, "xy", None),
        check_vma=False,
    )
```

```python
import functools

import jax
import jax.numpy as jnp
from jax import lax
from jax.experimental import pallas as pl
from jax.experimental.pallas import tpu as pltpu
from jax.sharding import PartitionSpec as P

NB = 128
NCLS = 8

h_diffusion = 0.2
v_diffusion = 0.2
step_duration = 0.5
collide_scale = 2.0

MESH = pl.DeviceIdType.MESH
SUB, LANE = 8, 128
RING = 4
GROUP = NB // RING
PIECES = 4
PART = GROUP // PIECES
QUADS = PART // 4
OFFSETS = (2, 1, 3, 0)
AUX = 3
SPAN = 8
BATCH = RING * QUADS * 2
MESSAGE = AUX + PIECES * BATCH
ALPHA = step_duration * collide_scale / NB


def turn(value, shift, axis):
    return pltpu.roll(value, shift % value.shape[axis], axis)


def swap_rows(a, b, c, d):
    sub = lax.broadcasted_iota(jnp.int32, (SUB, LANE), 0)
    even, low = sub % 2 == 0, sub % 4 < 2
    ab, ba = jnp.where(even, a, turn(b, 1, 0)), jnp.where(even, turn(a, -1, 0), b)
    cd, dc = jnp.where(even, c, turn(d, 1, 0)), jnp.where(even, turn(c, -1, 0), d)
    return (
        jnp.where(low, ab, turn(cd, 2, 0)),
        jnp.where(low, ba, turn(dc, 2, 0)),
        jnp.where(low, turn(ab, -2, 0), cd),
        jnp.where(low, turn(ba, -2, 0), dc),
    )


def step_kernel(
    depth,
    bands,
    conc_hbm,
    vel_x_hbm,
    vel_y_hbm,
    sea_mask_hbm,
    settle_hbm,
    classes_hbm,
    up_hbm,
    down_hbm,
    break_hbm,
    settled,
    tables,
    conc,
    vel_x,
    vel_y,
    sea_mask,
    settle,
    classes,
    up_table,
    down_table,
    break_table,
    up_out,
    down_out,
    up_in,
    down_in,
    moved,
    column,
    mixed,
    sinks,
    factors,
    load_sem,
    enter_sem,
    up_send,
    up_recv,
    down_send,
    down_recv,
    ring_send,
    ring_recv,
    deep_send,
    deep_recv,
    back_send,
    back_recv,
):
    place = lax.axis_index("bins")
    band = lax.axis_index("xy")
    z, x = place // RING, place % RING
    top, bottom = z == 0, z == depth - 1
    first_band, last_band = band == 0, band == bands - 1
    barrier = pltpu.get_barrier_semaphore()

    def greet(bins, xy):
        pl.semaphore_signal(barrier, inc=1, device_id=(bins, xy), device_id_type=MESH)

    for d in (1, 2, 3):
        greet(z * RING + (x + d) % RING, band)
    pl.when(~first_band)(lambda: greet(place, band - 1))
    pl.when(~last_band)(lambda: greet(place, band + 1))
    pl.when(~bottom)(lambda: greet(place + RING, band))

    loads = [
        pltpu.make_async_copy(src, dst, load_sem.at[i])
        for i, (src, dst) in enumerate(
            (
                (conc_hbm, conc),
                (vel_x_hbm, vel_x),
                (vel_y_hbm, vel_y),
                (sea_mask_hbm, sea_mask),
                (settle_hbm, settle),
                (classes_hbm, classes),
                (up_hbm, up_table),
                (down_hbm, down_table),
                (break_hbm, break_table),
            )
        )
    ]
    for copy in loads:
        copy.start()

    zero = jnp.zeros((SUB, LANE), jnp.float32)

    @pl.when(first_band)
    def _():
        down_in[...] = jnp.zeros_like(down_in)

    @pl.when(last_band)
    def _():
        up_in[...] = jnp.zeros_like(up_in)

    sub = lax.broadcasted_iota(jnp.int32, (SUB, LANE), 0)
    lane = lax.broadcasted_iota(jnp.int32, (SUB, LANE), 1)
    lane_first, lane_last = lane == 0, lane == LANE - 1
    half = sub < 4
    seam = (half & lane_first) | (~half & lane_last)

    for copy in loads:
        copy.wait()

    def plane(ref):
        whole = ref[...].reshape(4, 2 * LANE)
        return jnp.concatenate([whole[:, :LANE], whole[:, LANE:]], 0)

    fields = [
        swap_rows(*[value] * 4)
        for value in (plane(vel_x), plane(vel_y), plane(sea_mask).astype(jnp.float32))
    ]
    for k, rows in enumerate(fields):
        up_out[k] = rows[0]
        down_out[k] = rows[3]

    def pack(j):
        for n, d in enumerate(OFFSETS):
            for q in range(QUADS):
                first = (x + d) % RING * GROUP + j * PART + 4 * q
                rows = swap_rows(*[conc[first + i] for i in range(4)])
                spot = AUX + j * BATCH + (n * QUADS + q) * 2
                up_out[spot], up_out[spot + 1] = rows[0], rows[1]
                down_out[spot], down_out[spot + 1] = rows[2], rows[3]

    def halo(j, start, source, target, send, recv, to):
        rows = pl.ds(start + j * BATCH, BATCH + AUX - start)
        return pltpu.make_async_remote_copy(
            src_ref=source.at[rows],
            dst_ref=target.at[rows],
            send_sem=send,
            recv_sem=recv.at[j],
            device_id=(place, to),
            device_id_type=MESH,
        )

    def halo_up(j, start):
        return halo(j, start, up_out, up_in, up_send, up_recv, band - 1)

    def halo_down(j, start):
        return halo(j, start, down_out, down_in, down_send, down_recv, band + 1)

    def settle_bytes(ref, sem):
        pltpu.make_async_copy(ref, ref, sem).wait()

    def ring(j, d):
        return pltpu.make_async_remote_copy(
            src_ref=moved.at[d, pl.ds(j * PART, PART)],
            dst_ref=column.at[2 + x, pl.ds(j * PART, PART)],
            send_sem=ring_send,
            recv_sem=ring_recv.at[j],
            device_id=(z * RING + (x + d) % RING, band),
            device_id_type=MESH,
        )

    def deep_down(j):
        part = pl.ds(j * PART, PART)
        return pltpu.make_async_remote_copy(
            src_ref=column.at[pl.ds(4, 2), part],
            dst_ref=column.at[pl.ds(0, 2), part],
            send_sem=deep_send.at[0],
            recv_sem=deep_recv.at[j, 0],
            device_id=(place + RING, band),
            device_id_type=MESH,
        )

    def deep_up(j):
        part = pl.ds(j * PART, PART)
        return pltpu.make_async_remote_copy(
            src_ref=column.at[pl.ds(2, 2), part],
            dst_ref=column.at[pl.ds(6, 2), part],
            send_sem=deep_send.at[1],
            recv_sem=deep_recv.at[j, 1],
            device_id=(place - RING, band),
            device_id_type=MESH,
        )

    def back(j, level, source):
        part = pl.ds(j * PART, PART)
        return pltpu.make_async_remote_copy(
            src_ref=mixed.at[level, part],
            dst_ref=settled.at[source, part],
            send_sem=back_send,
            recv_sem=back_recv,
            device_id=(z * RING + level, band),
            device_id_type=MESH,
        )

    def send_halo(j, start):
        pl.when(~first_band)(lambda: halo_up(j, start).start())
        pl.when(~last_band)(lambda: halo_down(j, start).start())

    def take_halo(j, start):
        pl.when(~last_band)(lambda: halo_up(j, start).wait_recv())
        pl.when(~first_band)(lambda: halo_down(j, start).wait_recv())

    pack(0)
    greeted = 3 + (1 - first_band.astype(jnp.int32)) + (1 - last_band.astype(jnp.int32))
    pl.semaphore_wait(barrier, greeted + (1 - top.astype(jnp.int32)))
    send_halo(0, 0)

    @pl.when(~top)
    def _():
        pl.semaphore_signal(
            enter_sem, inc=1, device_id=(place - RING, band), device_id_type=MESH
        )

    def rest_pack(j, unused):
        pack(j)
        send_halo(j, AUX)
        return unused

    lax.fori_loop(1, PIECES, rest_pack, 0)

    def spread(value):
        return jnp.broadcast_to(value.reshape(1, NB), (NB, NB)).T

    own_class = classes[...].reshape(1, NB)
    bins = lax.broadcasted_iota(jnp.int32, (1, NB), 1)

    def lookup(table):
        value = jnp.zeros((1, NB), jnp.float32)
        for k in range(NCLS):
            value = jnp.where(own_class == k, table[k], value)
        return value

    rate = step_duration * lookup(break_table)
    tables[0] = spread(settle[...])
    for k in range(GROUP // SUB):
        sink = tables[0, pl.ds(pl.multiple_of(x * GROUP + k * SUB, SUB), SUB)]
        other = turn(sink, 4, 0)
        sinks[2 * k] = jnp.where(half, sink, other)
        sinks[2 * k + 1] = jnp.where(half, other, sink)
    tables[0] = spread(lookup(up_table))
    tables[1] = spread(lookup(down_table))
    tables[2] = spread(rate / jnp.maximum(bins, 1).astype(jnp.float32))
    tables[3] = spread(jnp.where(bins >= 1, 1.0 - rate, 1.0))

    def weights(spot, along, across, mask):
        factors[spot, 0] = (1.0 - 4.0 * h_diffusion) * mask
        factors[spot, 1] = mask * (h_diffusion - 0.5 * along)
        factors[spot, 2] = mask * (h_diffusion + 0.5 * along)
        factors[spot, 3] = mask * (h_diffusion - 0.5 * across)
        factors[spot, 4] = mask * (h_diffusion + 0.5 * across)

    for r in range(4):
        weights(1 + r, *[rows[r] for rows in fields])
    take_halo(0, 0)
    weights(0, *[down_in[k] for k in range(AUX)])
    weights(5, *[up_in[k] for k in range(AUX)])

    def transport(west, cells, east, spot):
        swapped = jnp.where(seam, turn(cells, 4, 0), 0.0)
        north = turn(jnp.where(lane_first, swapped, cells), -1, 1)
        south = turn(jnp.where(lane_last, swapped, cells), 1, 1)
        return (
            factors[spot, 0] * cells
            + factors[spot, 1] * east
            + factors[spot, 2] * west
            + factors[spot, 3] * north
            + factors[spot, 4] * south
        )

    def horizontal(j, unused):
        pl.when(j > 0)(lambda: take_halo(j, AUX))
        for n, d in enumerate(OFFSETS):
            for q in range(QUADS):
                spot = AUX + j * BATCH + (n * QUADS + q) * 2
                rows = [
                    ref[spot + i] for ref in (down_in, up_out, down_out, up_in) for i in (0, 1)
                ]
                once = [transport(*rows[r : r + 3], r) for r in range(6)]
                for r in range(4):
                    twice = transport(*once[r : r + 3], 1 + r)
                    if d:
                        moved[d, j * PART + 4 * q + r] = twice
                    else:
                        column[2 + x, j * PART + 4 * q + r] = twice
        for d in OFFSETS[:3]:
            ring(j, d).start()
        return unused

    lax.fori_loop(0, PIECES, horizontal, 0)
    pl.when(~bottom)(lambda: pl.semaphore_wait(enter_sem, 1))

    def forward(j):
        settle_bytes(column.at[pl.ds(2, 3), pl.ds(j * PART, PART)], ring_recv.at[j])
        pl.when(~top)(lambda: deep_up(j).start())
        pl.when(~bottom)(lambda: deep_down(j).start())

    def settle_mix(levels, sink, start):
        share = v_diffusion
        keep, fall = 1.0 - 2.0 * share - sink, share + sink
        fresh = []
        for k in range(len(levels) - 2):
            upper, own, lower = levels[k : k + 3]
            upper_term = fall * upper
            lower_term = share * lower
            if start + k == 2:
                upper_term = jnp.where(top, share * own, upper_term)
            if start + k == 5:
                lower_term = jnp.where(bottom, share * own, lower_term)
            fresh.append(keep * own + upper_term + lower_term)
        return fresh

    def vertical(j, first, wide):
        for q in range(QUADS):
            spot = j * PART + 4 * q
            sink = sinks[j * QUADS + q]
            rows = []
            for r in range(4):
                levels = [column[first - 2 + k, spot + r] for k in range(wide + 4)]
                rows.append(settle_mix(settle_mix(levels, sink, first - 1), sink, first))
            for k in range(wide):
                for r in range(4):
                    mixed[first - 2 + k, spot + r] = rows[r][k]
        for level in range(first - 2, first - 2 + wide):
            pl.when(x != level)(lambda level=level: back(j, level, x).start())

    def upper_half(j):
        pl.when(~top)(lambda: deep_down(j).wait_recv())
        vertical(j, 2, 2)

    def lower_half(j, unused):
        pl.when(~bottom)(lambda: deep_up(j).wait_recv())
        vertical(j, 4, 2)
        for i in range(PART):
            settled[x, j * PART + i] = mixed[x, j * PART + i]
        return unused

    forward(0)

    def middle(j, unused):
        forward(j)
        upper_half(j - 1)
        return unused

    lax.fori_loop(1, PIECES, middle, 0)
    upper_half(PIECES - 1)
    lax.fori_loop(0, PIECES, lower_half, 0)

    settle_bytes(settled.at[pl.ds(0, 3)], back_recv)
    settle_bytes(moved.at[pl.ds(1, 3)], ring_send)
    settle_bytes(mixed.at[pl.ds(0, 3)], back_send)
    pl.when(~top)(lambda: settle_bytes(column.at[pl.ds(2, 2)], deep_send.at[1]))
    pl.when(~bottom)(lambda: settle_bytes(column.at[pl.ds(4, 2)], deep_send.at[0]))
    pl.when(~first_band)(lambda: settle_bytes(up_out, up_send))
    pl.when(~last_band)(lambda: settle_bytes(down_out, down_send))


def collide_kernel(settled, tables, out_hbm, cells_by_bin, out, sums, out_sem):
    parts = NB // SPAN

    def row(k, b):
        return jnp.broadcast_to(tables[k, pl.ds(b, 1)], (SUB, LANE))

    def store(p):
        part = pl.ds(p * SPAN, SPAN)
        return pltpu.make_async_copy(out.at[part], out_hbm.at[part], out_sem.at[p])

    def total(p, unused):
        b = p * SPAN
        cells = []
        for q in range(0, SPAN, 4):
            cells += swap_rows(*[settled[b + q + r] for r in range(4)])
        for i in range(SPAN):
            cells_by_bin[b + i] = cells[i]
        for k in range(3):
            terms = [row(k, b + i) * cells[i] for i in range(SPAN)]
            while len(terms) > 1:
                terms = [one + two for one, two in zip(terms[::2], terms[1::2])]
            sums[k, p] = terms[0]
        return unused

    lax.fori_loop(0, parts, total, 0, unroll=2)
    lower = jnp.zeros((SUB, LANE), jnp.float32)
    for p in range(parts):
        own = sums[0, p]
        sums[0, p] = lower
        lower = lower + own
    for k in (1, 2):
        higher = jnp.zeros((SUB, LANE), jnp.float32)
        for p in reversed(range(parts)):
            higher = higher + sums[k, p]
            sums[k, p] = higher

    def collide(p, unused):
        lower, higher, pieces = sums[0, p], sums[1, p], sums[2, p]
        for i in range(SPAN):
            b = p * SPAN + i
            cells = cells_by_bin[b]
            loss, gain = row(0, b), row(1, b)
            higher = higher - gain * cells
            pieces = pieces - row(2, b) * cells
            out[b] = cells * (row(3, b) + ALPHA * (gain * lower - loss * higher)) + pieces
            lower = lower + loss * cells
        store(p).start()
        return unused

    lax.fori_loop(0, parts, collide, 0, unroll=2)

    def finish(p, unused):
        store(p).wait()
        return unused

    lax.fori_loop(0, parts, finish, 0)


def local(depth, bands, conc, *rest):
    cells = conc.reshape(NB, 4, 2, LANE).transpose(0, 2, 1, 3).reshape(NB, SUB, LANE)
    vmem = pl.BlockSpec(memory_space=pltpu.VMEM)
    dma = pltpu.SemaphoreType.DMA
    tile = (SUB, LANE)

    def buffer(*shape):
        return pltpu.VMEM(shape + tile, jnp.float32)

    settled, tables = pl.pallas_call(
        functools.partial(step_kernel, depth, bands),
        out_shape=(
            jax.ShapeDtypeStruct((RING, GROUP) + tile, jnp.float32),
            jax.ShapeDtypeStruct((4, NB, LANE), jnp.float32),
        ),
        in_specs=[pl.BlockSpec(memory_space=pltpu.HBM)] * 9,
        out_specs=(vmem, vmem),
        scratch_shapes=[
            buffer(NB),
            pltpu.VMEM((1, 4, 2 * LANE), jnp.float32),
            pltpu.VMEM((1, 4, 2 * LANE), jnp.float32),
            pltpu.VMEM((4, 2 * LANE), jnp.int32),
            pltpu.VMEM((NB,), jnp.float32),
            pltpu.VMEM((NB,), jnp.int32),
            pltpu.SMEM((NCLS,), jnp.float32),
            pltpu.SMEM((NCLS,), jnp.float32),
            pltpu.SMEM((NCLS,), jnp.float32),
            buffer(MESSAGE),
            buffer(MESSAGE),
            buffer(MESSAGE),
            buffer(MESSAGE),
            buffer(RING, GROUP),
            buffer(8, GROUP),
            buffer(RING, GROUP),
            buffer(GROUP // 4),
            buffer(6, 5),
            dma((9,)),
            pltpu.SemaphoreType.REGULAR,
            dma,
            dma((PIECES,)),
            dma,
            dma((PIECES,)),
            dma,
            dma((PIECES,)),
            dma((2,)),
            dma((PIECES, 2)),
            dma,
            dma,
        ],
        compiler_params=pltpu.CompilerParams(
            collective_id=0, has_side_effects=True, vmem_limit_bytes=20 << 20
        ),
    )(*[pltpu.with_memory_space_constraint(value, pltpu.HBM) for value in (cells, *rest)])
    result = pl.pallas_call(
        collide_kernel,
        out_shape=jax.ShapeDtypeStruct((NB,) + tile, jnp.float32),
        in_specs=[vmem, vmem],
        out_specs=pl.BlockSpec(memory_space=pl.ANY),
        scratch_shapes=[buffer(NB), buffer(NB), buffer(3, NB // SPAN), dma((NB // SPAN,))],
        compiler_params=pltpu.CompilerParams(vmem_limit_bytes=8 << 20),
    )(settled.reshape((NB,) + tile), tables)
    return result.reshape(NB, 2, 4, LANE).transpose(0, 2, 1, 3).reshape(conc.shape)


def solution(mesh):
    placed = (
        P("bins", None, "xy", None),
        P("bins", "xy", None),
        P("bins", "xy", None),
        P("xy", None),
        P(),
        P(),
        P(),
        P(),
        P(),
    )
    return jax.shard_map(
        functools.partial(local, mesh.shape["bins"] // RING, mesh.shape["xy"]),
        mesh=mesh,
        in_specs=placed,
        out_specs=P("bins", None, "xy", None),
        check_vma=False,
    )
```

```python
import functools

import jax
import jax.numpy as jnp
from jax import lax
from jax.experimental import pallas as pl
from jax.experimental.pallas import tpu as pltpu
from jax.sharding import PartitionSpec as P

NB = 128
NCLS = 8

h_diffusion = 0.2
v_diffusion = 0.2
step_duration = 0.5
collide_scale = 2.0

MESH = pl.DeviceIdType.MESH
SUB, LANE = 8, 128
RING = 4
GROUP = NB // RING
PIECES = 8
PART = GROUP // PIECES
QUADS = PART // 4
OFFSETS = (2, 1, 3, 0)
AUX = 3
SPAN = 8
BATCH = RING * QUADS * 2
MESSAGE = AUX + PIECES * BATCH
ALPHA = step_duration * collide_scale / NB


def turn(value, shift, axis):
    return pltpu.roll(value, shift % value.shape[axis], axis)


def swap_rows(a, b, c, d):
    sub = lax.broadcasted_iota(jnp.int32, (SUB, LANE), 0)
    even, low = sub % 2 == 0, sub % 4 < 2
    ab, ba = jnp.where(even, a, turn(b, 1, 0)), jnp.where(even, turn(a, -1, 0), b)
    cd, dc = jnp.where(even, c, turn(d, 1, 0)), jnp.where(even, turn(c, -1, 0), d)
    return (
        jnp.where(low, ab, turn(cd, 2, 0)),
        jnp.where(low, ba, turn(dc, 2, 0)),
        jnp.where(low, turn(ab, -2, 0), cd),
        jnp.where(low, turn(ba, -2, 0), dc),
    )


def step_kernel(
    depth,
    bands,
    conc_hbm,
    vel_x_hbm,
    vel_y_hbm,
    sea_mask_hbm,
    settle_hbm,
    classes_hbm,
    up_hbm,
    down_hbm,
    break_hbm,
    settled,
    tables,
    conc,
    vel_x,
    vel_y,
    sea_mask,
    settle,
    classes,
    up_table,
    down_table,
    break_table,
    up_out,
    down_out,
    up_in,
    down_in,
    moved,
    column,
    mixed,
    sinks,
    factors,
    load_sem,
    enter_sem,
    up_send,
    up_recv,
    down_send,
    down_recv,
    ring_send,
    ring_recv,
    deep_send,
    deep_recv,
    back_send,
    back_recv,
):
    place = lax.axis_index("bins")
    band = lax.axis_index("xy")
    z, x = place // RING, place % RING
    top, bottom = z == 0, z == depth - 1
    first_band, last_band = band == 0, band == bands - 1
    barrier = pltpu.get_barrier_semaphore()

    def greet(bins, xy):
        pl.semaphore_signal(barrier, inc=1, device_id=(bins, xy), device_id_type=MESH)

    for d in (1, 2, 3):
        greet(z * RING + (x + d) % RING, band)
    pl.when(~first_band)(lambda: greet(place, band - 1))
    pl.when(~last_band)(lambda: greet(place, band + 1))
    pl.when(~bottom)(lambda: greet(place + RING, band))

    loads = [
        pltpu.make_async_copy(src, dst, load_sem.at[i])
        for i, (src, dst) in enumerate(
            (
                (conc_hbm, conc),
                (vel_x_hbm, vel_x),
                (vel_y_hbm, vel_y),
                (sea_mask_hbm, sea_mask),
                (settle_hbm, settle),
                (classes_hbm, classes),
                (up_hbm, up_table),
                (down_hbm, down_table),
                (break_hbm, break_table),
            )
        )
    ]
    for copy in loads:
        copy.start()

    zero = jnp.zeros((SUB, LANE), jnp.float32)

    @pl.when(first_band)
    def _():
        down_in[...] = jnp.zeros_like(down_in)

    @pl.when(last_band)
    def _():
        up_in[...] = jnp.zeros_like(up_in)

    sub = lax.broadcasted_iota(jnp.int32, (SUB, LANE), 0)
    lane = lax.broadcasted_iota(jnp.int32, (SUB, LANE), 1)
    lane_first, lane_last = lane == 0, lane == LANE - 1
    half = sub < 4
    seam = (half & lane_first) | (~half & lane_last)

    for copy in loads:
        copy.wait()

    def plane(ref):
        whole = ref[...].reshape(4, 2 * LANE)
        return jnp.concatenate([whole[:, :LANE], whole[:, LANE:]], 0)

    fields = [
        swap_rows(*[value] * 4)
        for value in (plane(vel_x), plane(vel_y), plane(sea_mask).astype(jnp.float32))
    ]
    for k, rows in enumerate(fields):
        up_out[k] = rows[0]
        down_out[k] = rows[3]

    def pack(j):
        for n, d in enumerate(OFFSETS):
            for q in range(QUADS):
                first = (x + d) % RING * GROUP + j * PART + 4 * q
                rows = swap_rows(*[conc[first + i] for i in range(4)])
                spot = AUX + j * BATCH + (n * QUADS + q) * 2
                up_out[spot], up_out[spot + 1] = rows[0], rows[1]
                down_out[spot], down_out[spot + 1] = rows[2], rows[3]

    def halo(j, start, source, target, send, recv, to):
        rows = pl.ds(start + j * BATCH, BATCH + AUX - start)
        return pltpu.make_async_remote_copy(
            src_ref=source.at[rows],
            dst_ref=target.at[rows],
            send_sem=send,
            recv_sem=recv.at[j],
            device_id=(place, to),
            device_id_type=MESH,
        )

    def halo_up(j, start):
        return halo(j, start, up_out, up_in, up_send, up_recv, band - 1)

    def halo_down(j, start):
        return halo(j, start, down_out, down_in, down_send, down_recv, band + 1)

    def settle_bytes(ref, sem):
        pltpu.make_async_copy(ref, ref, sem).wait()

    def ring(j, d):
        return pltpu.make_async_remote_copy(
            src_ref=moved.at[d, pl.ds(j * PART, PART)],
            dst_ref=column.at[2 + x, pl.ds(j * PART, PART)],
            send_sem=ring_send,
            recv_sem=ring_recv.at[j],
            device_id=(z * RING + (x + d) % RING, band),
            device_id_type=MESH,
        )

    def deep_down(j):
        part = pl.ds(j * PART, PART)
        return pltpu.make_async_remote_copy(
            src_ref=column.at[pl.ds(4, 2), part],
            dst_ref=column.at[pl.ds(0, 2), part],
            send_sem=deep_send.at[0],
            recv_sem=deep_recv.at[j, 0],
            device_id=(place + RING, band),
            device_id_type=MESH,
        )

    def deep_up(j):
        part = pl.ds(j * PART, PART)
        return pltpu.make_async_remote_copy(
            src_ref=column.at[pl.ds(2, 2), part],
            dst_ref=column.at[pl.ds(6, 2), part],
            send_sem=deep_send.at[1],
            recv_sem=deep_recv.at[j, 1],
            device_id=(place - RING, band),
            device_id_type=MESH,
        )

    def back(j, level, source):
        part = pl.ds(j * PART, PART)
        return pltpu.make_async_remote_copy(
            src_ref=mixed.at[level, part],
            dst_ref=settled.at[source, part],
            send_sem=back_send,
            recv_sem=back_recv,
            device_id=(z * RING + level, band),
            device_id_type=MESH,
        )

    def send_halo(j, start):
        pl.when(~first_band)(lambda: halo_up(j, start).start())
        pl.when(~last_band)(lambda: halo_down(j, start).start())

    def take_halo(j, start):
        pl.when(~last_band)(lambda: halo_up(j, start).wait_recv())
        pl.when(~first_band)(lambda: halo_down(j, start).wait_recv())

    pack(0)
    greeted = 3 + (1 - first_band.astype(jnp.int32)) + (1 - last_band.astype(jnp.int32))
    pl.semaphore_wait(barrier, greeted + (1 - top.astype(jnp.int32)))
    send_halo(0, 0)

    @pl.when(~top)
    def _():
        pl.semaphore_signal(
            enter_sem, inc=1, device_id=(place - RING, band), device_id_type=MESH
        )

    def rest_pack(j, unused):
        pack(j)
        send_halo(j, AUX)
        return unused

    lax.fori_loop(1, PIECES, rest_pack, 0)

    def spread(value):
        return jnp.broadcast_to(value.reshape(1, NB), (NB, NB)).T

    own_class = classes[...].reshape(1, NB)
    bins = lax.broadcasted_iota(jnp.int32, (1, NB), 1)

    def lookup(table):
        value = jnp.zeros((1, NB), jnp.float32)
        for k in range(NCLS):
            value = jnp.where(own_class == k, table[k], value)
        return value

    rate = step_duration * lookup(break_table)
    tables[0] = spread(settle[...])
    for k in range(GROUP // SUB):
        sink = tables[0, pl.ds(pl.multiple_of(x * GROUP + k * SUB, SUB), SUB)]
        other = turn(sink, 4, 0)
        sinks[2 * k] = jnp.where(half, sink, other)
        sinks[2 * k + 1] = jnp.where(half, other, sink)
    tables[0] = spread(lookup(up_table))
    tables[1] = spread(lookup(down_table))
    tables[2] = spread(rate / jnp.maximum(bins, 1).astype(jnp.float32))
    tables[3] = spread(jnp.where(bins >= 1, 1.0 - rate, 1.0))

    def weights(spot, along, across, mask):
        factors[spot, 0] = (1.0 - 4.0 * h_diffusion) * mask
        factors[spot, 1] = mask * (h_diffusion - 0.5 * along)
        factors[spot, 2] = mask * (h_diffusion + 0.5 * along)
        factors[spot, 3] = mask * (h_diffusion - 0.5 * across)
        factors[spot, 4] = mask * (h_diffusion + 0.5 * across)

    for r in range(4):
        weights(1 + r, *[rows[r] for rows in fields])
    take_halo(0, 0)
    weights(0, *[down_in[k] for k in range(AUX)])
    weights(5, *[up_in[k] for k in range(AUX)])

    def transport(west, cells, east, spot):
        swapped = jnp.where(seam, turn(cells, 4, 0), 0.0)
        north = turn(jnp.where(lane_first, swapped, cells), -1, 1)
        south = turn(jnp.where(lane_last, swapped, cells), 1, 1)
        return (
            factors[spot, 0] * cells
            + factors[spot, 1] * east
            + factors[spot, 2] * west
            + factors[spot, 3] * north
            + factors[spot, 4] * south
        )

    def horizontal(j, unused):
        pl.when(j > 0)(lambda: take_halo(j, AUX))
        for n, d in enumerate(OFFSETS):
            for q in range(QUADS):
                spot = AUX + j * BATCH + (n * QUADS + q) * 2
                rows = [
                    ref[spot + i] for ref in (down_in, up_out, down_out, up_in) for i in (0, 1)
                ]
                once = [transport(*rows[r : r + 3], r) for r in range(6)]
                for r in range(4):
                    twice = transport(*once[r : r + 3], 1 + r)
                    if d:
                        moved[d, j * PART + 4 * q + r] = twice
                    else:
                        column[2 + x, j * PART + 4 * q + r] = twice
        for d in OFFSETS[:3]:
            ring(j, d).start()
        return unused

    lax.fori_loop(0, PIECES, horizontal, 0)
    pl.when(~bottom)(lambda: pl.semaphore_wait(enter_sem, 1))

    def forward(j):
        settle_bytes(column.at[pl.ds(2, 3), pl.ds(j * PART, PART)], ring_recv.at[j])
        pl.when(~top)(lambda: deep_up(j).start())
        pl.when(~bottom)(lambda: deep_down(j).start())

    def settle_mix(levels, sink, start):
        share = v_diffusion
        keep, fall = 1.0 - 2.0 * share - sink, share + sink
        fresh = []
        for k in range(len(levels) - 2):
            upper, own, lower = levels[k : k + 3]
            upper_term = fall * upper
            lower_term = share * lower
            if start + k == 2:
                upper_term = jnp.where(top, share * own, upper_term)
            if start + k == 5:
                lower_term = jnp.where(bottom, share * own, lower_term)
            fresh.append(keep * own + upper_term + lower_term)
        return fresh

    def vertical(j, first, wide):
        for q in range(QUADS):
            spot = j * PART + 4 * q
            sink = sinks[j * QUADS + q]
            rows = []
            for r in range(4):
                levels = [column[first - 2 + k, spot + r] for k in range(wide + 4)]
                rows.append(settle_mix(settle_mix(levels, sink, first - 1), sink, first))
            for k in range(wide):
                for r in range(4):
                    mixed[first - 2 + k, spot + r] = rows[r][k]
        for level in range(first - 2, first - 2 + wide):
            pl.when(x != level)(lambda level=level: back(j, level, x).start())

    def upper_half(j):
        pl.when(~top)(lambda: deep_down(j).wait_recv())
        vertical(j, 2, 2)

    def lower_half(j):
        pl.when(~bottom)(lambda: deep_up(j).wait_recv())
        vertical(j, 4, 2)
        for i in range(PART):
            settled[x, j * PART + i] = mixed[x, j * PART + i]

    def follow(lead, lag):
        for j in range(lead):
            forward(j)
        for j in range(PIECES + lag):
            if j < PIECES:
                upper_half(j)
            if j >= lag:
                lower_half(j - lag)
            if lead + j < PIECES:
                forward(lead + j)

    corner = band < 2
    together = (z > depth // 2) | (top & corner)
    apart = ~together & ~((z == 1) & corner)
    pl.when(together)(lambda: follow(5, 0))
    pl.when(apart)(lambda: follow(5, 4))
    pl.when(~together & ~apart)(lambda: follow(PIECES, 0))

    settle_bytes(settled.at[pl.ds(0, 3)], back_recv)
    settle_bytes(moved.at[pl.ds(1, 3)], ring_send)
    settle_bytes(mixed.at[pl.ds(0, 3)], back_send)
    pl.when(~top)(lambda: settle_bytes(column.at[pl.ds(2, 2)], deep_send.at[1]))
    pl.when(~bottom)(lambda: settle_bytes(column.at[pl.ds(4, 2)], deep_send.at[0]))
    pl.when(~first_band)(lambda: settle_bytes(up_out, up_send))
    pl.when(~last_band)(lambda: settle_bytes(down_out, down_send))


def collide_kernel(settled, tables, out_hbm, cells_by_bin, out, sums, out_sem):
    parts = NB // SPAN

    def row(k, b):
        return jnp.broadcast_to(tables[k, pl.ds(b, 1)], (SUB, LANE))

    def store(p):
        part = pl.ds(p * SPAN, SPAN)
        return pltpu.make_async_copy(out.at[part], out_hbm.at[part], out_sem.at[p])

    def total(p, unused):
        b = p * SPAN
        cells = []
        for q in range(0, SPAN, 4):
            cells += swap_rows(*[settled[b + q + r] for r in range(4)])
        for i in range(SPAN):
            cells_by_bin[b + i] = cells[i]
        for k in range(3):
            terms = [row(k, b + i) * cells[i] for i in range(SPAN)]
            while len(terms) > 1:
                terms = [one + two for one, two in zip(terms[::2], terms[1::2])]
            sums[k, p] = terms[0]
        return unused

    lax.fori_loop(0, parts, total, 0, unroll=2)
    lower = jnp.zeros((SUB, LANE), jnp.float32)
    for p in range(parts):
        own = sums[0, p]
        sums[0, p] = lower
        lower = lower + own
    for k in (1, 2):
        higher = jnp.zeros((SUB, LANE), jnp.float32)
        for p in reversed(range(parts)):
            higher = higher + sums[k, p]
            sums[k, p] = higher

    def collide(p, unused):
        lower, higher, pieces = sums[0, p], sums[1, p], sums[2, p]
        for i in range(SPAN):
            b = p * SPAN + i
            cells = cells_by_bin[b]
            loss, gain = row(0, b), row(1, b)
            higher = higher - gain * cells
            pieces = pieces - row(2, b) * cells
            out[b] = cells * (row(3, b) + ALPHA * (gain * lower - loss * higher)) + pieces
            lower = lower + loss * cells
        store(p).start()
        return unused

    lax.fori_loop(0, parts, collide, 0, unroll=2)

    def finish(p, unused):
        store(p).wait()
        return unused

    lax.fori_loop(0, parts, finish, 0)


def local(depth, bands, conc, *rest):
    cells = conc.reshape(NB, 4, 2, LANE).transpose(0, 2, 1, 3).reshape(NB, SUB, LANE)
    vmem = pl.BlockSpec(memory_space=pltpu.VMEM)
    dma = pltpu.SemaphoreType.DMA
    tile = (SUB, LANE)

    def buffer(*shape):
        return pltpu.VMEM(shape + tile, jnp.float32)

    settled, tables = pl.pallas_call(
        functools.partial(step_kernel, depth, bands),
        out_shape=(
            jax.ShapeDtypeStruct((RING, GROUP) + tile, jnp.float32),
            jax.ShapeDtypeStruct((4, NB, LANE), jnp.float32),
        ),
        in_specs=[pl.BlockSpec(memory_space=pltpu.HBM)] * 9,
        out_specs=(vmem, vmem),
        scratch_shapes=[
            buffer(NB),
            pltpu.VMEM((1, 4, 2 * LANE), jnp.float32),
            pltpu.VMEM((1, 4, 2 * LANE), jnp.float32),
            pltpu.VMEM((4, 2 * LANE), jnp.int32),
            pltpu.VMEM((NB,), jnp.float32),
            pltpu.VMEM((NB,), jnp.int32),
            pltpu.SMEM((NCLS,), jnp.float32),
            pltpu.SMEM((NCLS,), jnp.float32),
            pltpu.SMEM((NCLS,), jnp.float32),
            buffer(MESSAGE),
            buffer(MESSAGE),
            buffer(MESSAGE),
            buffer(MESSAGE),
            buffer(RING, GROUP),
            buffer(8, GROUP),
            buffer(RING, GROUP),
            buffer(GROUP // 4),
            buffer(6, 5),
            dma((9,)),
            pltpu.SemaphoreType.REGULAR,
            dma,
            dma((PIECES,)),
            dma,
            dma((PIECES,)),
            dma,
            dma((PIECES,)),
            dma((2,)),
            dma((PIECES, 2)),
            dma,
            dma,
        ],
        compiler_params=pltpu.CompilerParams(
            collective_id=0, has_side_effects=True, vmem_limit_bytes=20 << 20
        ),
    )(*[pltpu.with_memory_space_constraint(value, pltpu.HBM) for value in (cells, *rest)])
    result = pl.pallas_call(
        collide_kernel,
        out_shape=jax.ShapeDtypeStruct((NB,) + tile, jnp.float32),
        in_specs=[vmem, vmem],
        out_specs=pl.BlockSpec(memory_space=pl.ANY),
        scratch_shapes=[buffer(NB), buffer(NB), buffer(3, NB // SPAN), dma((NB // SPAN,))],
        compiler_params=pltpu.CompilerParams(vmem_limit_bytes=8 << 20),
    )(settled.reshape((NB,) + tile), tables)
    return result.reshape(NB, 2, 4, LANE).transpose(0, 2, 1, 3).reshape(conc.shape)


def solution(mesh):
    placed = (
        P("bins", None, "xy", None),
        P("bins", "xy", None),
        P("bins", "xy", None),
        P("xy", None),
        P(),
        P(),
        P(),
        P(),
        P(),
    )
    return jax.shard_map(
        functools.partial(local, mesh.shape["bins"] // RING, mesh.shape["xy"]),
        mesh=mesh,
        in_specs=placed,
        out_specs=P("bins", None, "xy", None),
        check_vma=False,
    )
```

```python
import functools

import jax
import jax.numpy as jnp
from jax import lax
from jax.experimental import pallas as pl
from jax.experimental.pallas import tpu as pltpu
from jax.sharding import PartitionSpec as P

NB = 128
NCLS = 8

h_diffusion = 0.2
v_diffusion = 0.2
step_duration = 0.5
collide_scale = 2.0

MESH = pl.DeviceIdType.MESH
SUB, LANE = 8, 128
RING = 4
GROUP = NB // RING
PIECES = 8
PART = GROUP // PIECES
QUADS = PART // 4
OFFSETS = (2, 1, 3, 0)
AUX = 3
SPAN = 8
BATCH = RING * QUADS * 2
MESSAGE = AUX + PIECES * BATCH
ALPHA = step_duration * collide_scale / NB


def turn(value, shift, axis):
    return pltpu.roll(value, shift % value.shape[axis], axis)


def swap_rows(a, b, c, d):
    sub = lax.broadcasted_iota(jnp.int32, (SUB, LANE), 0)
    even, low = sub % 2 == 0, sub % 4 < 2
    ab, ba = jnp.where(even, a, turn(b, 1, 0)), jnp.where(even, turn(a, -1, 0), b)
    cd, dc = jnp.where(even, c, turn(d, 1, 0)), jnp.where(even, turn(c, -1, 0), d)
    return (
        jnp.where(low, ab, turn(cd, 2, 0)),
        jnp.where(low, ba, turn(dc, 2, 0)),
        jnp.where(low, turn(ab, -2, 0), cd),
        jnp.where(low, turn(ba, -2, 0), dc),
    )


def step_kernel(
    depth,
    bands,
    conc_hbm,
    vel_x_hbm,
    vel_y_hbm,
    sea_mask_hbm,
    settle_hbm,
    classes_hbm,
    up_hbm,
    down_hbm,
    break_hbm,
    settled,
    tables,
    conc,
    vel_x,
    vel_y,
    sea_mask,
    settle,
    classes,
    up_table,
    down_table,
    break_table,
    up_out,
    down_out,
    up_in,
    down_in,
    moved,
    column,
    mixed,
    sinks,
    factors,
    load_sem,
    enter_sem,
    higher_sem,
    up_send,
    up_recv,
    down_send,
    down_recv,
    ring_send,
    ring_recv,
    deep_send,
    deep_recv,
    back_send,
    back_recv,
):
    place = lax.axis_index("bins")
    band = lax.axis_index("xy")
    z, x = place // RING, place % RING
    top, bottom = z == 0, z == depth - 1
    first_band, last_band = band == 0, band == bands - 1
    barrier = pltpu.get_barrier_semaphore()

    def greet(bins, xy):
        pl.semaphore_signal(barrier, inc=1, device_id=(bins, xy), device_id_type=MESH)

    pl.when(~first_band)(lambda: greet(place, band - 1))
    pl.when(~last_band)(lambda: greet(place, band + 1))
    for d in (1, 2, 3):
        pl.when(x < RING - d)(lambda d=d: greet(place + d, band))
    pl.when(~bottom)(lambda: greet(place + RING, band))

    loads = [
        pltpu.make_async_copy(src, dst, load_sem.at[i])
        for i, (src, dst) in enumerate(
            (
                (conc_hbm, conc),
                (vel_x_hbm, vel_x),
                (vel_y_hbm, vel_y),
                (sea_mask_hbm, sea_mask),
                (settle_hbm, settle),
                (classes_hbm, classes),
                (up_hbm, up_table),
                (down_hbm, down_table),
                (break_hbm, break_table),
            )
        )
    ]
    for copy in loads:
        copy.start()

    zero = jnp.zeros((SUB, LANE), jnp.float32)

    @pl.when(first_band)
    def _():
        down_in[...] = jnp.zeros_like(down_in)

    @pl.when(last_band)
    def _():
        up_in[...] = jnp.zeros_like(up_in)

    sub = lax.broadcasted_iota(jnp.int32, (SUB, LANE), 0)
    lane = lax.broadcasted_iota(jnp.int32, (SUB, LANE), 1)
    lane_first, lane_last = lane == 0, lane == LANE - 1
    half = sub < 4
    seam = (half & lane_first) | (~half & lane_last)

    for copy in loads:
        copy.wait()

    def plane(ref):
        whole = ref[...].reshape(4, 2 * LANE)
        return jnp.concatenate([whole[:, :LANE], whole[:, LANE:]], 0)

    fields = [
        swap_rows(*[value] * 4)
        for value in (plane(vel_x), plane(vel_y), plane(sea_mask).astype(jnp.float32))
    ]
    for k, rows in enumerate(fields):
        up_out[k] = rows[0]
        down_out[k] = rows[3]

    def pack(j):
        for n, d in enumerate(OFFSETS):
            for q in range(QUADS):
                first = (x + d) % RING * GROUP + j * PART + 4 * q
                rows = swap_rows(*[conc[first + i] for i in range(4)])
                spot = AUX + j * BATCH + (n * QUADS + q) * 2
                up_out[spot], up_out[spot + 1] = rows[0], rows[1]
                down_out[spot], down_out[spot + 1] = rows[2], rows[3]

    def halo(j, start, source, target, send, recv, to):
        rows = pl.ds(start + j * BATCH, BATCH + AUX - start)
        return pltpu.make_async_remote_copy(
            src_ref=source.at[rows],
            dst_ref=target.at[rows],
            send_sem=send,
            recv_sem=recv.at[j],
            device_id=(place, to),
            device_id_type=MESH,
        )

    def halo_up(j, start):
        return halo(j, start, up_out, up_in, up_send, up_recv, band - 1)

    def halo_down(j, start):
        return halo(j, start, down_out, down_in, down_send, down_recv, band + 1)

    def settle_bytes(ref, sem):
        pltpu.make_async_copy(ref, ref, sem).wait()

    def ring(j, d):
        return pltpu.make_async_remote_copy(
            src_ref=moved.at[d, pl.ds(j * PART, PART)],
            dst_ref=column.at[2 + x, pl.ds(j * PART, PART)],
            send_sem=ring_send,
            recv_sem=ring_recv.at[j],
            device_id=(z * RING + (x + d) % RING, band),
            device_id_type=MESH,
        )

    def deep_down(j):
        part = pl.ds(j * PART, PART)
        return pltpu.make_async_remote_copy(
            src_ref=column.at[pl.ds(4, 2), part],
            dst_ref=column.at[pl.ds(0, 2), part],
            send_sem=deep_send.at[0],
            recv_sem=deep_recv.at[j, 0],
            device_id=(place + RING, band),
            device_id_type=MESH,
        )

    def deep_up(j):
        part = pl.ds(j * PART, PART)
        return pltpu.make_async_remote_copy(
            src_ref=column.at[pl.ds(2, 2), part],
            dst_ref=column.at[pl.ds(6, 2), part],
            send_sem=deep_send.at[1],
            recv_sem=deep_recv.at[j, 1],
            device_id=(place - RING, band),
            device_id_type=MESH,
        )

    def back(j, level, source):
        part = pl.ds(j * PART, PART)
        return pltpu.make_async_remote_copy(
            src_ref=mixed.at[level, part],
            dst_ref=settled.at[source, part],
            send_sem=back_send,
            recv_sem=back_recv,
            device_id=(z * RING + level, band),
            device_id_type=MESH,
        )

    def send_halo(j, start):
        pl.when(~first_band)(lambda: halo_up(j, start).start())
        pl.when(~last_band)(lambda: halo_down(j, start).start())

    def take_halo(j, start):
        pl.when(~last_band)(lambda: halo_up(j, start).wait_recv())
        pl.when(~first_band)(lambda: halo_down(j, start).wait_recv())

    pack(0)
    greeted = x + (1 - first_band.astype(jnp.int32)) + (1 - last_band.astype(jnp.int32))
    pl.semaphore_wait(barrier, greeted + (1 - top.astype(jnp.int32)))
    send_halo(0, 0)

    @pl.when(~top)
    def _():
        pl.semaphore_signal(
            enter_sem, inc=1, device_id=(place - RING, band), device_id_type=MESH
        )

    for d in (1, 2, 3):

        @pl.when(x >= d)
        def _(d=d):
            pl.semaphore_signal(
                higher_sem, inc=1, device_id=(place - d, band), device_id_type=MESH
            )

    def rest_pack(j, unused):
        pack(j)
        send_halo(j, AUX)
        return unused

    lax.fori_loop(1, PIECES, rest_pack, 0)

    def spread(value):
        return jnp.broadcast_to(value.reshape(1, NB), (NB, NB)).T

    own_class = classes[...].reshape(1, NB)
    bins = lax.broadcasted_iota(jnp.int32, (1, NB), 1)

    def lookup(table):
        value = jnp.zeros((1, NB), jnp.float32)
        for k in range(NCLS):
            value = jnp.where(own_class == k, table[k], value)
        return value

    rate = step_duration * lookup(break_table)
    tables[0] = spread(settle[...])
    for k in range(GROUP // SUB):
        sink = tables[0, pl.ds(pl.multiple_of(x * GROUP + k * SUB, SUB), SUB)]
        other = turn(sink, 4, 0)
        sinks[2 * k] = jnp.where(half, sink, other)
        sinks[2 * k + 1] = jnp.where(half, other, sink)
    tables[0] = spread(lookup(up_table))
    tables[1] = spread(lookup(down_table))
    tables[2] = spread(rate / jnp.maximum(bins, 1).astype(jnp.float32))
    tables[3] = spread(jnp.where(bins >= 1, 1.0 - rate, 1.0))

    def weights(spot, along, across, mask):
        factors[spot, 0] = (1.0 - 4.0 * h_diffusion) * mask
        factors[spot, 1] = mask * (h_diffusion - 0.5 * along)
        factors[spot, 2] = mask * (h_diffusion + 0.5 * along)
        factors[spot, 3] = mask * (h_diffusion - 0.5 * across)
        factors[spot, 4] = mask * (h_diffusion + 0.5 * across)

    for r in range(4):
        weights(1 + r, *[rows[r] for rows in fields])
    take_halo(0, 0)
    weights(0, *[down_in[k] for k in range(AUX)])
    weights(5, *[up_in[k] for k in range(AUX)])

    def transport(west, cells, east, spot):
        swapped = jnp.where(seam, turn(cells, 4, 0), 0.0)
        north = turn(jnp.where(lane_first, swapped, cells), -1, 1)
        south = turn(jnp.where(lane_last, swapped, cells), 1, 1)
        return (
            factors[spot, 0] * cells
            + factors[spot, 1] * east
            + factors[spot, 2] * west
            + factors[spot, 3] * north
            + factors[spot, 4] * south
        )

    def horizontal(j, unused):
        pl.when(j > 0)(lambda: take_halo(j, AUX))
        for n, d in enumerate(OFFSETS):
            for q in range(QUADS):
                spot = AUX + j * BATCH + (n * QUADS + q) * 2
                rows = [
                    ref[spot + i] for ref in (down_in, up_out, down_out, up_in) for i in (0, 1)
                ]
                once = [transport(*rows[r : r + 3], r) for r in range(6)]
                for r in range(4):
                    twice = transport(*once[r : r + 3], 1 + r)
                    if d:
                        moved[d, j * PART + 4 * q + r] = twice
                    else:
                        column[2 + x, j * PART + 4 * q + r] = twice
        pl.when((j == 0) & (x < RING - 1))(lambda: pl.semaphore_wait(higher_sem, RING - 1 - x))
        for d in OFFSETS[:3]:
            ring(j, d).start()
        return unused

    lax.fori_loop(0, PIECES, horizontal, 0)
    pl.when(~bottom)(lambda: pl.semaphore_wait(enter_sem, 1))

    def forward(j):
        settle_bytes(column.at[pl.ds(2, 3), pl.ds(j * PART, PART)], ring_recv.at[j])
        pl.when(~top)(lambda: deep_up(j).start())
        pl.when(~bottom)(lambda: deep_down(j).start())

    def settle_mix(levels, sink, start):
        share = v_diffusion
        keep, fall = 1.0 - 2.0 * share - sink, share + sink
        fresh = []
        for k in range(len(levels) - 2):
            upper, own, lower = levels[k : k + 3]
            upper_term = fall * upper
            lower_term = share * lower
            if start + k == 2:
                upper_term = jnp.where(top, share * own, upper_term)
            if start + k == 5:
                lower_term = jnp.where(bottom, share * own, lower_term)
            fresh.append(keep * own + upper_term + lower_term)
        return fresh

    def vertical(j, first, wide):
        for q in range(QUADS):
            spot = j * PART + 4 * q
            sink = sinks[j * QUADS + q]
            rows = []
            for r in range(4):
                levels = [column[first - 2 + k, spot + r] for k in range(wide + 4)]
                rows.append(settle_mix(settle_mix(levels, sink, first - 1), sink, first))
            for k in range(wide):
                for r in range(4):
                    mixed[first - 2 + k, spot + r] = rows[r][k]
        for level in range(first - 2, first - 2 + wide):
            pl.when(x != level)(lambda level=level: back(j, level, x).start())

    def upper_half(j):
        pl.when(~top)(lambda: deep_down(j).wait_recv())
        vertical(j, 2, 2)

    def lower_half(j):
        pl.when(~bottom)(lambda: deep_up(j).wait_recv())
        vertical(j, 4, 2)
        for i in range(PART):
            settled[x, j * PART + i] = mixed[x, j * PART + i]

    def follow(lead, lag):
        for j in range(lead):
            forward(j)
        for j in range(PIECES + lag):
            if j < PIECES:
                upper_half(j)
            if j >= lag:
                lower_half(j - lag)
            if lead + j < PIECES:
                forward(lead + j)

    corner = band < 2
    together = (z > depth // 2) | (top & corner)
    apart = ~together & ~((z == 1) & corner)
    pl.when(together)(lambda: follow(4, 1))
    pl.when(apart)(lambda: follow(6, 3))
    pl.when(~together & ~apart)(lambda: follow(PIECES, 0))

    settle_bytes(settled.at[pl.ds(0, 3)], back_recv)
    settle_bytes(moved.at[pl.ds(1, 3)], ring_send)
    settle_bytes(mixed.at[pl.ds(0, 3)], back_send)
    pl.when(~top)(lambda: settle_bytes(column.at[pl.ds(2, 2)], deep_send.at[1]))
    pl.when(~bottom)(lambda: settle_bytes(column.at[pl.ds(4, 2)], deep_send.at[0]))
    pl.when(~first_band)(lambda: settle_bytes(up_out, up_send))
    pl.when(~last_band)(lambda: settle_bytes(down_out, down_send))


def collide_kernel(settled, tables, out_hbm, cells_by_bin, out, sums, out_sem):
    parts = NB // SPAN

    def row(k, b):
        return jnp.broadcast_to(tables[k, pl.ds(b, 1)], (SUB, LANE))

    def store(p):
        part = pl.ds(p * SPAN, SPAN)
        return pltpu.make_async_copy(out.at[part], out_hbm.at[part], out_sem.at[p])

    def total(p, unused):
        b = p * SPAN
        cells = []
        for q in range(0, SPAN, 4):
            cells += swap_rows(*[settled[b + q + r] for r in range(4)])
        for i in range(SPAN):
            cells_by_bin[b + i] = cells[i]
        for k in range(3):
            terms = [row(k, b + i) * cells[i] for i in range(SPAN)]
            while len(terms) > 1:
                terms = [one + two for one, two in zip(terms[::2], terms[1::2])]
            sums[k, p] = terms[0]
        return unused

    lax.fori_loop(0, parts, total, 0, unroll=4)
    lower = jnp.zeros((SUB, LANE), jnp.float32)
    for p in range(parts):
        own = sums[0, p]
        sums[0, p] = lower
        lower = lower + own
    for k in (1, 2):
        higher = jnp.zeros((SUB, LANE), jnp.float32)
        for p in reversed(range(parts)):
            higher = higher + sums[k, p]
            sums[k, p] = higher

    def collide(p, unused):
        lower, higher, pieces = sums[0, p], sums[1, p], sums[2, p]
        for i in range(SPAN):
            b = p * SPAN + i
            cells = cells_by_bin[b]
            loss, gain = row(0, b), row(1, b)
            higher = higher - gain * cells
            pieces = pieces - row(2, b) * cells
            out[b] = cells * (row(3, b) + ALPHA * (gain * lower - loss * higher)) + pieces
            lower = lower + loss * cells
        store(p).start()
        return unused

    lax.fori_loop(0, parts, collide, 0, unroll=4)

    def finish(p, unused):
        store(p).wait()
        return unused

    lax.fori_loop(0, parts, finish, 0)


def local(depth, bands, conc, *rest):
    cells = conc.reshape(NB, 4, 2, LANE).transpose(0, 2, 1, 3).reshape(NB, SUB, LANE)
    vmem = pl.BlockSpec(memory_space=pltpu.VMEM)
    dma = pltpu.SemaphoreType.DMA
    tile = (SUB, LANE)

    def buffer(*shape):
        return pltpu.VMEM(shape + tile, jnp.float32)

    settled, tables = pl.pallas_call(
        functools.partial(step_kernel, depth, bands),
        out_shape=(
            jax.ShapeDtypeStruct((RING, GROUP) + tile, jnp.float32),
            jax.ShapeDtypeStruct((4, NB, LANE), jnp.float32),
        ),
        in_specs=[pl.BlockSpec(memory_space=pltpu.HBM)] * 9,
        out_specs=(vmem, vmem),
        scratch_shapes=[
            buffer(NB),
            pltpu.VMEM((1, 4, 2 * LANE), jnp.float32),
            pltpu.VMEM((1, 4, 2 * LANE), jnp.float32),
            pltpu.VMEM((4, 2 * LANE), jnp.int32),
            pltpu.VMEM((NB,), jnp.float32),
            pltpu.VMEM((NB,), jnp.int32),
            pltpu.SMEM((NCLS,), jnp.float32),
            pltpu.SMEM((NCLS,), jnp.float32),
            pltpu.SMEM((NCLS,), jnp.float32),
            buffer(MESSAGE),
            buffer(MESSAGE),
            buffer(MESSAGE),
            buffer(MESSAGE),
            buffer(RING, GROUP),
            buffer(8, GROUP),
            buffer(RING, GROUP),
            buffer(GROUP // 4),
            buffer(6, 5),
            dma((9,)),
            pltpu.SemaphoreType.REGULAR,
            pltpu.SemaphoreType.REGULAR,
            dma,
            dma((PIECES,)),
            dma,
            dma((PIECES,)),
            dma,
            dma((PIECES,)),
            dma((2,)),
            dma((PIECES, 2)),
            dma,
            dma,
        ],
        compiler_params=pltpu.CompilerParams(
            collective_id=0, has_side_effects=True, vmem_limit_bytes=20 << 20
        ),
    )(*[pltpu.with_memory_space_constraint(value, pltpu.HBM) for value in (cells, *rest)])
    result = pl.pallas_call(
        collide_kernel,
        out_shape=jax.ShapeDtypeStruct((NB,) + tile, jnp.float32),
        in_specs=[vmem, vmem],
        out_specs=pl.BlockSpec(memory_space=pl.ANY),
        scratch_shapes=[buffer(NB), buffer(NB), buffer(3, NB // SPAN), dma((NB // SPAN,))],
        compiler_params=pltpu.CompilerParams(vmem_limit_bytes=8 << 20),
    )(settled.reshape((NB,) + tile), tables)
    return result.reshape(NB, 2, 4, LANE).transpose(0, 2, 1, 3).reshape(conc.shape)


def solution(mesh):
    placed = (
        P("bins", None, "xy", None),
        P("bins", "xy", None),
        P("bins", "xy", None),
        P("xy", None),
        P(),
        P(),
        P(),
        P(),
        P(),
    )
    return jax.shard_map(
        functools.partial(local, mesh.shape["bins"] // RING, mesh.shape["xy"]),
        mesh=mesh,
        in_specs=placed,
        out_specs=P("bins", None, "xy", None),
        check_vma=False,
    )
```

```python
import functools

import jax
import jax.numpy as jnp
from jax import lax
from jax.experimental import pallas as pl
from jax.experimental.pallas import tpu as pltpu
from jax.sharding import PartitionSpec as P

NB = 128
NCLS = 8

h_diffusion = 0.2
v_diffusion = 0.2
step_duration = 0.5
collide_scale = 2.0

MESH = pl.DeviceIdType.MESH
SUB, LANE = 8, 128
RING = 4
GROUP = NB // RING
PIECES = 8
PART = GROUP // PIECES
QUADS = PART // 4
OFFSETS = (2, 1, 3, 0)
AUX = 3
SPAN = 8
AHEAD = 1
BATCH = RING * QUADS * 2
MESSAGE = AUX + PIECES * BATCH
ALPHA = step_duration * collide_scale / NB


def turn(value, shift, axis):
    return pltpu.roll(value, shift % value.shape[axis], axis)


def swap_rows(a, b, c, d):
    sub = lax.broadcasted_iota(jnp.int32, (SUB, LANE), 0)
    even, low = sub % 2 == 0, sub % 4 < 2
    ab, ba = jnp.where(even, a, turn(b, 1, 0)), jnp.where(even, turn(a, -1, 0), b)
    cd, dc = jnp.where(even, c, turn(d, 1, 0)), jnp.where(even, turn(c, -1, 0), d)
    return (
        jnp.where(low, ab, turn(cd, 2, 0)),
        jnp.where(low, ba, turn(dc, 2, 0)),
        jnp.where(low, turn(ab, -2, 0), cd),
        jnp.where(low, turn(ba, -2, 0), dc),
    )


def step_kernel(
    depth,
    bands,
    conc_hbm,
    vel_x_hbm,
    vel_y_hbm,
    sea_mask_hbm,
    settle_hbm,
    classes_hbm,
    up_hbm,
    down_hbm,
    break_hbm,
    settled,
    tables,
    conc,
    vel_x,
    vel_y,
    sea_mask,
    settle,
    classes,
    up_table,
    down_table,
    break_table,
    up_out,
    down_out,
    up_in,
    down_in,
    moved,
    column,
    mixed,
    sinks,
    factors,
    load_sem,
    enter_sem,
    higher_sem,
    up_send,
    up_recv,
    down_send,
    down_recv,
    ring_send,
    ring_recv,
    deep_send,
    deep_recv,
    back_send,
    back_recv,
):
    place = lax.axis_index("bins")
    band = lax.axis_index("xy")
    z, x = place // RING, place % RING
    top, bottom = z == 0, z == depth - 1
    first_band, last_band = band == 0, band == bands - 1
    barrier = pltpu.get_barrier_semaphore()

    def greet(bins, xy):
        pl.semaphore_signal(barrier, inc=1, device_id=(bins, xy), device_id_type=MESH)

    pl.when(~first_band)(lambda: greet(place, band - 1))
    pl.when(~last_band)(lambda: greet(place, band + 1))
    for d in (1, 2, 3):
        pl.when(x < RING - d)(lambda d=d: greet(place + d, band))
    pl.when(~bottom)(lambda: greet(place + RING, band))

    loads = [
        pltpu.make_async_copy(src, dst, load_sem.at[i])
        for i, (src, dst) in enumerate(
            (
                (conc_hbm, conc),
                (vel_x_hbm, vel_x),
                (vel_y_hbm, vel_y),
                (sea_mask_hbm, sea_mask),
                (settle_hbm, settle),
                (classes_hbm, classes),
                (up_hbm, up_table),
                (down_hbm, down_table),
                (break_hbm, break_table),
            )
        )
    ]
    for copy in loads:
        copy.start()

    zero = jnp.zeros((SUB, LANE), jnp.float32)

    @pl.when(first_band)
    def _():
        down_in[...] = jnp.zeros_like(down_in)

    @pl.when(last_band)
    def _():
        up_in[...] = jnp.zeros_like(up_in)

    sub = lax.broadcasted_iota(jnp.int32, (SUB, LANE), 0)
    lane = lax.broadcasted_iota(jnp.int32, (SUB, LANE), 1)
    lane_first, lane_last = lane == 0, lane == LANE - 1
    half = sub < 4
    seam = (half & lane_first) | (~half & lane_last)

    for copy in loads:
        copy.wait()

    def plane(ref):
        whole = ref[...].reshape(4, 2 * LANE)
        return jnp.concatenate([whole[:, :LANE], whole[:, LANE:]], 0)

    fields = [
        swap_rows(*[value] * 4)
        for value in (plane(vel_x), plane(vel_y), plane(sea_mask).astype(jnp.float32))
    ]
    for k, rows in enumerate(fields):
        up_out[k] = rows[0]
        down_out[k] = rows[3]

    def pack(j):
        for n, d in enumerate(OFFSETS):
            for q in range(QUADS):
                first = (x + d) % RING * GROUP + j * PART + 4 * q
                rows = swap_rows(*[conc[first + i] for i in range(4)])
                spot = AUX + j * BATCH + (n * QUADS + q) * 2
                up_out[spot], up_out[spot + 1] = rows[0], rows[1]
                down_out[spot], down_out[spot + 1] = rows[2], rows[3]

    def halo(j, start, source, target, send, recv, to):
        rows = pl.ds(start + j * BATCH, BATCH + AUX - start)
        return pltpu.make_async_remote_copy(
            src_ref=source.at[rows],
            dst_ref=target.at[rows],
            send_sem=send,
            recv_sem=recv.at[j],
            device_id=(place, to),
            device_id_type=MESH,
        )

    def halo_up(j, start):
        return halo(j, start, up_out, up_in, up_send, up_recv, band - 1)

    def halo_down(j, start):
        return halo(j, start, down_out, down_in, down_send, down_recv, band + 1)

    def settle_bytes(ref, sem):
        pltpu.make_async_copy(ref, ref, sem).wait()

    def ring(j, d):
        return pltpu.make_async_remote_copy(
            src_ref=moved.at[d, pl.ds(j * PART, PART)],
            dst_ref=column.at[2 + x, pl.ds(j * PART, PART)],
            send_sem=ring_send,
            recv_sem=ring_recv.at[j, x // 2],
            device_id=(z * RING + (x + d) % RING, band),
            device_id_type=MESH,
        )

    def deep_down(j):
        part = pl.ds(j * PART, PART)
        return pltpu.make_async_remote_copy(
            src_ref=column.at[pl.ds(4, 2), part],
            dst_ref=column.at[pl.ds(0, 2), part],
            send_sem=deep_send.at[0],
            recv_sem=deep_recv.at[j, 0],
            device_id=(place + RING, band),
            device_id_type=MESH,
        )

    def deep_up(j):
        part = pl.ds(j * PART, PART)
        return pltpu.make_async_remote_copy(
            src_ref=column.at[pl.ds(2, 2), part],
            dst_ref=column.at[pl.ds(6, 2), part],
            send_sem=deep_send.at[1],
            recv_sem=deep_recv.at[j, 1],
            device_id=(place - RING, band),
            device_id_type=MESH,
        )

    def back(j, level, source):
        part = pl.ds(j * PART, PART)
        return pltpu.make_async_remote_copy(
            src_ref=mixed.at[level, part],
            dst_ref=settled.at[source, part],
            send_sem=back_send,
            recv_sem=back_recv,
            device_id=(z * RING + level, band),
            device_id_type=MESH,
        )

    def send_halo(j, start):
        pl.when(~first_band)(lambda: halo_up(j, start).start())
        pl.when(~last_band)(lambda: halo_down(j, start).start())

    def take_halo(j, start):
        pl.when(~last_band)(lambda: halo_up(j, start).wait_recv())
        pl.when(~first_band)(lambda: halo_down(j, start).wait_recv())

    pack(0)
    greeted = x + (1 - first_band.astype(jnp.int32)) + (1 - last_band.astype(jnp.int32))
    pl.semaphore_wait(barrier, greeted + (1 - top.astype(jnp.int32)))
    send_halo(0, 0)

    @pl.when(~top)
    def _():
        pl.semaphore_signal(
            enter_sem, inc=1, device_id=(place - RING, band), device_id_type=MESH
        )

    for d in (1, 2, 3):

        @pl.when(x >= d)
        def _(d=d):
            pl.semaphore_signal(
                higher_sem, inc=1, device_id=(place - d, band), device_id_type=MESH
            )

    def rest_pack(j, unused):
        pack(j)
        send_halo(j, AUX)
        return unused

    lax.fori_loop(1, PIECES, rest_pack, 0)

    def spread(value):
        return jnp.broadcast_to(value.reshape(1, NB), (NB, NB)).T

    own_class = classes[...].reshape(1, NB)
    bins = lax.broadcasted_iota(jnp.int32, (1, NB), 1)

    def lookup(table):
        value = jnp.zeros((1, NB), jnp.float32)
        for k in range(NCLS):
            value = jnp.where(own_class == k, table[k], value)
        return value

    rate = step_duration * lookup(break_table)
    tables[0] = spread(settle[...])
    for k in range(GROUP // SUB):
        sink = tables[0, pl.ds(pl.multiple_of(x * GROUP + k * SUB, SUB), SUB)]
        other = turn(sink, 4, 0)
        sinks[2 * k] = jnp.where(half, sink, other)
        sinks[2 * k + 1] = jnp.where(half, other, sink)
    tables[0] = spread(lookup(up_table))
    tables[1] = spread(lookup(down_table))
    tables[2] = spread(rate / jnp.maximum(bins, 1).astype(jnp.float32))
    tables[3] = spread(jnp.where(bins >= 1, 1.0 - rate, 1.0))

    def weights(spot, along, across, mask):
        factors[spot, 0] = (1.0 - 4.0 * h_diffusion) * mask
        factors[spot, 1] = mask * (h_diffusion - 0.5 * along)
        factors[spot, 2] = mask * (h_diffusion + 0.5 * along)
        factors[spot, 3] = mask * (h_diffusion - 0.5 * across)
        factors[spot, 4] = mask * (h_diffusion + 0.5 * across)

    for r in range(4):
        weights(1 + r, *[rows[r] for rows in fields])
    take_halo(0, 0)
    weights(0, *[down_in[k] for k in range(AUX)])
    weights(5, *[up_in[k] for k in range(AUX)])

    def transport(west, cells, east, spot):
        swapped = jnp.where(seam, turn(cells, 4, 0), 0.0)
        north = turn(jnp.where(lane_first, swapped, cells), -1, 1)
        south = turn(jnp.where(lane_last, swapped, cells), 1, 1)
        return (
            factors[spot, 0] * cells
            + factors[spot, 1] * east
            + factors[spot, 2] * west
            + factors[spot, 3] * north
            + factors[spot, 4] * south
        )

    def horizontal(j, unused):
        pl.when(j > 0)(lambda: take_halo(j, AUX))
        for n, d in enumerate(OFFSETS):
            for q in range(QUADS):
                spot = AUX + j * BATCH + (n * QUADS + q) * 2
                rows = [
                    ref[spot + i] for ref in (down_in, up_out, down_out, up_in) for i in (0, 1)
                ]
                once = [transport(*rows[r : r + 3], r) for r in range(6)]
                for r in range(4):
                    twice = transport(*once[r : r + 3], 1 + r)
                    if d:
                        moved[d, j * PART + 4 * q + r] = twice
                    else:
                        column[2 + x, j * PART + 4 * q + r] = twice
        pl.when((j == 0) & (x < RING - 1))(lambda: pl.semaphore_wait(higher_sem, RING - 1 - x))
        for d in OFFSETS[:3]:
            ring(j, d).start()
        return unused

    lax.fori_loop(0, PIECES, horizontal, 0)
    pl.when(~bottom)(lambda: pl.semaphore_wait(enter_sem, 1))

    def arrived(j, pair):
        own = x // 2 == pair
        for mine, count in ((own, 1), (~own, 2)):
            part = column.at[pl.ds(2, count), pl.ds(j * PART, PART)]
            pl.when(mine)(lambda part=part: settle_bytes(part, ring_recv.at[j, pair]))

    def forward_up(j):
        arrived(j, 0)
        pl.when(~top)(lambda: deep_up(j).start())

    def forward(j):
        for k in range(AHEAD + 1) if j == 0 else (j + AHEAD,):
            if k < PIECES:
                forward_up(k)
        arrived(j, 1)
        pl.when(~bottom)(lambda: deep_down(j).start())

    def settle_mix(levels, sink, start):
        share = v_diffusion
        keep, fall = 1.0 - 2.0 * share - sink, share + sink
        fresh = []
        for k in range(len(levels) - 2):
            upper, own, lower = levels[k : k + 3]
            upper_term = fall * upper
            lower_term = share * lower
            if start + k == 2:
                upper_term = jnp.where(top, share * own, upper_term)
            if start + k == 5:
                lower_term = jnp.where(bottom, share * own, lower_term)
            fresh.append(keep * own + upper_term + lower_term)
        return fresh

    def vertical(j, first, wide):
        for q in range(QUADS):
            spot = j * PART + 4 * q
            sink = sinks[j * QUADS + q]
            rows = []
            for r in range(4):
                levels = [column[first - 2 + k, spot + r] for k in range(wide + 4)]
                rows.append(settle_mix(settle_mix(levels, sink, first - 1), sink, first))
            for k in range(wide):
                for r in range(4):
                    mixed[first - 2 + k, spot + r] = rows[r][k]
        for level in range(first - 2, first - 2 + wide):
            pl.when(x != level)(lambda level=level: back(j, level, x).start())

    def upper_half(j):
        pl.when(~top)(lambda: deep_down(j).wait_recv())
        vertical(j, 2, 2)

    def lower_half(j):
        pl.when(~bottom)(lambda: deep_up(j).wait_recv())
        vertical(j, 4, 2)
        for i in range(PART):
            settled[x, j * PART + i] = mixed[x, j * PART + i]

    def follow(lead, lag):
        for j in range(lead):
            forward(j)
        for j in range(PIECES + lag):
            if j < PIECES:
                upper_half(j)
            if j >= lag:
                lower_half(j - lag)
            if lead + j < PIECES:
                forward(lead + j)

    corner = band < 2
    together = (z > depth // 2) | (top & corner)
    apart = ~together & ~((z == 1) & corner)
    pl.when(together)(lambda: follow(4, 1))
    pl.when(apart)(lambda: follow(6, 2))
    pl.when(~together & ~apart)(lambda: follow(PIECES, 0))

    settle_bytes(settled.at[pl.ds(0, 3)], back_recv)
    settle_bytes(moved.at[pl.ds(1, 3)], ring_send)
    settle_bytes(mixed.at[pl.ds(0, 3)], back_send)
    pl.when(~top)(lambda: settle_bytes(column.at[pl.ds(2, 2)], deep_send.at[1]))
    pl.when(~bottom)(lambda: settle_bytes(column.at[pl.ds(4, 2)], deep_send.at[0]))
    pl.when(~first_band)(lambda: settle_bytes(up_out, up_send))
    pl.when(~last_band)(lambda: settle_bytes(down_out, down_send))


def collide_kernel(settled, tables, out_hbm, cells_by_bin, out, sums, out_sem):
    parts = NB // SPAN

    def row(k, b):
        return jnp.broadcast_to(tables[k, pl.ds(b, 1)], (SUB, LANE))

    def store(p):
        part = pl.ds(p * SPAN, SPAN)
        return pltpu.make_async_copy(out.at[part], out_hbm.at[part], out_sem.at[p])

    def total(p, unused):
        b = p * SPAN
        cells = []
        for q in range(0, SPAN, 4):
            cells += swap_rows(*[settled[b + q + r] for r in range(4)])
        for i in range(SPAN):
            cells_by_bin[b + i] = cells[i]
        for k in range(3):
            terms = [row(k, b + i) * cells[i] for i in range(SPAN)]
            while len(terms) > 1:
                terms = [one + two for one, two in zip(terms[::2], terms[1::2])]
            sums[k, p] = terms[0]
        return unused

    lax.fori_loop(0, parts, total, 0, unroll=4)
    lower = jnp.zeros((SUB, LANE), jnp.float32)
    for p in range(parts):
        own = sums[0, p]
        sums[0, p] = lower
        lower = lower + own
    for k in (1, 2):
        higher = jnp.zeros((SUB, LANE), jnp.float32)
        for p in reversed(range(parts)):
            higher = higher + sums[k, p]
            sums[k, p] = higher

    def collide(p, unused):
        lower, higher, pieces = sums[0, p], sums[1, p], sums[2, p]
        for i in range(SPAN):
            b = p * SPAN + i
            cells = cells_by_bin[b]
            loss, gain = row(0, b), row(1, b)
            higher = higher - gain * cells
            pieces = pieces - row(2, b) * cells
            out[b] = cells * (row(3, b) + ALPHA * (gain * lower - loss * higher)) + pieces
            lower = lower + loss * cells
        store(p).start()
        return unused

    lax.fori_loop(0, parts, collide, 0, unroll=4)

    def finish(p, unused):
        store(p).wait()
        return unused

    lax.fori_loop(0, parts, finish, 0)


def local(depth, bands, conc, *rest):
    cells = conc.reshape(NB, 4, 2, LANE).transpose(0, 2, 1, 3).reshape(NB, SUB, LANE)
    vmem = pl.BlockSpec(memory_space=pltpu.VMEM)
    dma = pltpu.SemaphoreType.DMA
    tile = (SUB, LANE)

    def buffer(*shape):
        return pltpu.VMEM(shape + tile, jnp.float32)

    settled, tables = pl.pallas_call(
        functools.partial(step_kernel, depth, bands),
        out_shape=(
            jax.ShapeDtypeStruct((RING, GROUP) + tile, jnp.float32),
            jax.ShapeDtypeStruct((4, NB, LANE), jnp.float32),
        ),
        in_specs=[pl.BlockSpec(memory_space=pltpu.HBM)] * 9,
        out_specs=(vmem, vmem),
        scratch_shapes=[
            buffer(NB),
            pltpu.VMEM((1, 4, 2 * LANE), jnp.float32),
            pltpu.VMEM((1, 4, 2 * LANE), jnp.float32),
            pltpu.VMEM((4, 2 * LANE), jnp.int32),
            pltpu.VMEM((NB,), jnp.float32),
            pltpu.VMEM((NB,), jnp.int32),
            pltpu.SMEM((NCLS,), jnp.float32),
            pltpu.SMEM((NCLS,), jnp.float32),
            pltpu.SMEM((NCLS,), jnp.float32),
            buffer(MESSAGE),
            buffer(MESSAGE),
            buffer(MESSAGE),
            buffer(MESSAGE),
            buffer(RING, GROUP),
            buffer(8, GROUP),
            buffer(RING, GROUP),
            buffer(GROUP // 4),
            buffer(6, 5),
            dma((9,)),
            pltpu.SemaphoreType.REGULAR,
            pltpu.SemaphoreType.REGULAR,
            dma,
            dma((PIECES,)),
            dma,
            dma((PIECES,)),
            dma,
            dma((PIECES, 2)),
            dma((2,)),
            dma((PIECES, 2)),
            dma,
            dma,
        ],
        compiler_params=pltpu.CompilerParams(
            collective_id=0, has_side_effects=True, vmem_limit_bytes=20 << 20
        ),
    )(*[pltpu.with_memory_space_constraint(value, pltpu.HBM) for value in (cells, *rest)])
    result = pl.pallas_call(
        collide_kernel,
        out_shape=jax.ShapeDtypeStruct((NB,) + tile, jnp.float32),
        in_specs=[vmem, vmem],
        out_specs=pl.BlockSpec(memory_space=pl.ANY),
        scratch_shapes=[buffer(NB), buffer(NB), buffer(3, NB // SPAN), dma((NB // SPAN,))],
        compiler_params=pltpu.CompilerParams(vmem_limit_bytes=8 << 20),
    )(settled.reshape((NB,) + tile), tables)
    return result.reshape(NB, 2, 4, LANE).transpose(0, 2, 1, 3).reshape(conc.shape)


def solution(mesh):
    placed = (
        P("bins", None, "xy", None),
        P("bins", "xy", None),
        P("bins", "xy", None),
        P("xy", None),
        P(),
        P(),
        P(),
        P(),
        P(),
    )
    return jax.shard_map(
        functools.partial(local, mesh.shape["bins"] // RING, mesh.shape["xy"]),
        mesh=mesh,
        in_specs=placed,
        out_specs=P("bins", None, "xy", None),
        check_vma=False,
    )
```

```python
import functools

import jax
import jax.numpy as jnp
from jax import lax
from jax.experimental import pallas as pl
from jax.experimental.pallas import tpu as pltpu
from jax.sharding import PartitionSpec as P

NB = 128
NCLS = 8

h_diffusion = 0.2
v_diffusion = 0.2
step_duration = 0.5
collide_scale = 2.0

MESH = pl.DeviceIdType.MESH
SUB, LANE = 8, 128
RING = 4
GROUP = NB // RING
PIECES = 8
PART = GROUP // PIECES
QUADS = PART // 4
OFFSETS = (2, 1, 3, 0)
AUX = 3
SPAN = 8
AHEAD = 1
BATCH = RING * QUADS * 2
MESSAGE = AUX + PIECES * BATCH
ALPHA = step_duration * collide_scale / NB


def turn(value, shift, axis):
    return pltpu.roll(value, shift % value.shape[axis], axis)


def swap_rows(a, b, c, d):
    sub = lax.broadcasted_iota(jnp.int32, (SUB, LANE), 0)
    even, low = sub % 2 == 0, sub % 4 < 2
    ab, ba = jnp.where(even, a, turn(b, 1, 0)), jnp.where(even, turn(a, -1, 0), b)
    cd, dc = jnp.where(even, c, turn(d, 1, 0)), jnp.where(even, turn(c, -1, 0), d)
    return (
        jnp.where(low, ab, turn(cd, 2, 0)),
        jnp.where(low, ba, turn(dc, 2, 0)),
        jnp.where(low, turn(ab, -2, 0), cd),
        jnp.where(low, turn(ba, -2, 0), dc),
    )


def step_kernel(
    depth,
    bands,
    conc_hbm,
    vel_x_hbm,
    vel_y_hbm,
    sea_mask_hbm,
    settle_hbm,
    classes_hbm,
    up_hbm,
    down_hbm,
    break_hbm,
    settled,
    tables,
    conc,
    vel_x,
    vel_y,
    sea_mask,
    settle,
    classes,
    up_table,
    down_table,
    break_table,
    up_out,
    down_out,
    up_in,
    down_in,
    moved,
    column,
    mixed,
    sinks,
    factors,
    load_sem,
    enter_sem,
    higher_sem,
    up_send,
    up_recv,
    down_send,
    down_recv,
    ring_send,
    ring_recv,
    deep_send,
    deep_recv,
    back_send,
    back_recv,
):
    place = lax.axis_index("bins")
    band = lax.axis_index("xy")
    z, x = place // RING, place % RING
    top, bottom = z == 0, z == depth - 1
    first_band, last_band = band == 0, band == bands - 1
    barrier = pltpu.get_barrier_semaphore()

    def greet(bins, xy):
        pl.semaphore_signal(barrier, inc=1, device_id=(bins, xy), device_id_type=MESH)

    pl.when(~first_band)(lambda: greet(place, band - 1))
    pl.when(~last_band)(lambda: greet(place, band + 1))
    for d in (1, 2, 3):
        pl.when(x < RING - d)(lambda d=d: greet(place + d, band))
    pl.when(~bottom)(lambda: greet(place + RING, band))

    loads = [
        pltpu.make_async_copy(src, dst, load_sem.at[i])
        for i, (src, dst) in enumerate(
            (
                (conc_hbm, conc),
                (vel_x_hbm, vel_x),
                (vel_y_hbm, vel_y),
                (sea_mask_hbm, sea_mask),
                (settle_hbm, settle),
                (classes_hbm, classes),
                (up_hbm, up_table),
                (down_hbm, down_table),
                (break_hbm, break_table),
            )
        )
    ]
    for copy in loads:
        copy.start()

    zero = jnp.zeros((SUB, LANE), jnp.float32)

    @pl.when(first_band)
    def _():
        down_in[...] = jnp.zeros_like(down_in)

    @pl.when(last_band)
    def _():
        up_in[...] = jnp.zeros_like(up_in)

    sub = lax.broadcasted_iota(jnp.int32, (SUB, LANE), 0)
    lane = lax.broadcasted_iota(jnp.int32, (SUB, LANE), 1)
    lane_first, lane_last = lane == 0, lane == LANE - 1
    half = sub < 4
    seam = (half & lane_first) | (~half & lane_last)

    for copy in loads:
        copy.wait()

    def plane(ref):
        whole = ref[...].reshape(4, 2 * LANE)
        return jnp.concatenate([whole[:, :LANE], whole[:, LANE:]], 0)

    fields = [
        swap_rows(*[value] * 4)
        for value in (plane(vel_x), plane(vel_y), plane(sea_mask).astype(jnp.float32))
    ]
    for k, rows in enumerate(fields):
        up_out[k] = rows[0]
        down_out[k] = rows[3]

    def pack(j):
        for n, d in enumerate(OFFSETS):
            for q in range(QUADS):
                first = (x + d) % RING * GROUP + j * PART + 4 * q
                rows = swap_rows(*[conc[first + i] for i in range(4)])
                spot = AUX + j * BATCH + (n * QUADS + q) * 2
                up_out[spot], up_out[spot + 1] = rows[0], rows[1]
                down_out[spot], down_out[spot + 1] = rows[2], rows[3]

    def halo(j, start, source, target, send, recv, to):
        rows = pl.ds(start + j * BATCH, BATCH + AUX - start)
        return pltpu.make_async_remote_copy(
            src_ref=source.at[rows],
            dst_ref=target.at[rows],
            send_sem=send,
            recv_sem=recv.at[j],
            device_id=(place, to),
            device_id_type=MESH,
        )

    def halo_up(j, start):
        return halo(j, start, up_out, up_in, up_send, up_recv, band - 1)

    def halo_down(j, start):
        return halo(j, start, down_out, down_in, down_send, down_recv, band + 1)

    def settle_bytes(ref, sem):
        pltpu.make_async_copy(ref, ref, sem).wait()

    def ring(j, d):
        return pltpu.make_async_remote_copy(
            src_ref=moved.at[d, pl.ds(j * PART, PART)],
            dst_ref=column.at[2 + x, pl.ds(j * PART, PART)],
            send_sem=ring_send,
            recv_sem=ring_recv.at[j, x // 2],
            device_id=(z * RING + (x + d) % RING, band),
            device_id_type=MESH,
        )

    def deep_down(j):
        part = pl.ds(j * PART, PART)
        return pltpu.make_async_remote_copy(
            src_ref=column.at[pl.ds(4, 2), part],
            dst_ref=column.at[pl.ds(0, 2), part],
            send_sem=deep_send.at[0],
            recv_sem=deep_recv.at[j, 0],
            device_id=(place + RING, band),
            device_id_type=MESH,
        )

    def deep_up(j):
        part = pl.ds(j * PART, PART)
        return pltpu.make_async_remote_copy(
            src_ref=column.at[pl.ds(2, 2), part],
            dst_ref=column.at[pl.ds(6, 2), part],
            send_sem=deep_send.at[1],
            recv_sem=deep_recv.at[j, 1],
            device_id=(place - RING, band),
            device_id_type=MESH,
        )

    def back(j, level, source):
        part = pl.ds(j * PART, PART)
        return pltpu.make_async_remote_copy(
            src_ref=mixed.at[level, part],
            dst_ref=settled.at[source, part],
            send_sem=back_send,
            recv_sem=back_recv,
            device_id=(z * RING + level, band),
            device_id_type=MESH,
        )

    def send_halo(j, start):
        pl.when(~first_band)(lambda: halo_up(j, start).start())
        pl.when(~last_band)(lambda: halo_down(j, start).start())

    def take_halo(j, start):
        pl.when(~last_band)(lambda: halo_up(j, start).wait_recv())
        pl.when(~first_band)(lambda: halo_down(j, start).wait_recv())

    pack(0)
    greeted = x + (1 - first_band.astype(jnp.int32)) + (1 - last_band.astype(jnp.int32))
    pl.semaphore_wait(barrier, greeted + (1 - top.astype(jnp.int32)))
    send_halo(0, 0)

    @pl.when(~top)
    def _():
        pl.semaphore_signal(
            enter_sem, inc=1, device_id=(place - RING, band), device_id_type=MESH
        )

    for d in (1, 2, 3):

        @pl.when(x >= d)
        def _(d=d):
            pl.semaphore_signal(
                higher_sem, inc=1, device_id=(place - d, band), device_id_type=MESH
            )

    def rest_pack(j, unused):
        pack(j)
        send_halo(j, AUX)
        return unused

    lax.fori_loop(1, PIECES, rest_pack, 0)

    def spread(value):
        return jnp.broadcast_to(value.reshape(1, NB), (NB, NB)).T

    own_class = classes[...].reshape(1, NB)
    bins = lax.broadcasted_iota(jnp.int32, (1, NB), 1)

    def lookup(table):
        value = jnp.zeros((1, NB), jnp.float32)
        for k in range(NCLS):
            value = jnp.where(own_class == k, table[k], value)
        return value

    rate = step_duration * lookup(break_table)
    tables[0] = spread(settle[...])
    for k in range(GROUP // SUB):
        sink = tables[0, pl.ds(pl.multiple_of(x * GROUP + k * SUB, SUB), SUB)]
        other = turn(sink, 4, 0)
        sinks[2 * k] = jnp.where(half, sink, other)
        sinks[2 * k + 1] = jnp.where(half, other, sink)
    tables[0] = spread(lookup(up_table))
    tables[1] = spread(lookup(down_table))
    tables[2] = spread(rate / jnp.maximum(bins, 1).astype(jnp.float32))
    tables[3] = spread(jnp.where(bins >= 1, 1.0 - rate, 1.0))

    def weights(spot, along, across, mask):
        factors[spot, 0] = (1.0 - 4.0 * h_diffusion) * mask
        factors[spot, 1] = mask * (h_diffusion - 0.5 * along)
        factors[spot, 2] = mask * (h_diffusion + 0.5 * along)
        factors[spot, 3] = mask * (h_diffusion - 0.5 * across)
        factors[spot, 4] = mask * (h_diffusion + 0.5 * across)

    for r in range(4):
        weights(1 + r, *[rows[r] for rows in fields])
    take_halo(0, 0)
    weights(0, *[down_in[k] for k in range(AUX)])
    weights(5, *[up_in[k] for k in range(AUX)])

    def transport(west, cells, east, spot):
        swapped = jnp.where(seam, turn(cells, 4, 0), 0.0)
        north = turn(jnp.where(lane_first, swapped, cells), -1, 1)
        south = turn(jnp.where(lane_last, swapped, cells), 1, 1)
        return (
            factors[spot, 0] * cells
            + factors[spot, 1] * east
            + factors[spot, 2] * west
            + factors[spot, 3] * north
            + factors[spot, 4] * south
        )

    def horizontal(j, unused):
        pl.when(j > 0)(lambda: take_halo(j, AUX))
        for n, d in enumerate(OFFSETS):
            for q in range(QUADS):
                spot = AUX + j * BATCH + (n * QUADS + q) * 2
                rows = [
                    ref[spot + i] for ref in (down_in, up_out, down_out, up_in) for i in (0, 1)
                ]
                once = [transport(*rows[r : r + 3], r) for r in range(6)]
                for r in range(4):
                    twice = transport(*once[r : r + 3], 1 + r)
                    if d:
                        moved[d, j * PART + 4 * q + r] = twice
                    else:
                        column[2 + x, j * PART + 4 * q + r] = twice
        pl.when((j == 0) & (x < RING - 1))(lambda: pl.semaphore_wait(higher_sem, RING - 1 - x))
        for d in OFFSETS[:3]:
            ring(j, d).start()
        return unused

    lax.fori_loop(0, PIECES, horizontal, 0)
    pl.when(~bottom)(lambda: pl.semaphore_wait(enter_sem, 1))

    def arrived(j, pair):
        own = x // 2 == pair
        for mine, count in ((own, 1), (~own, 2)):
            part = column.at[pl.ds(2, count), pl.ds(j * PART, PART)]
            pl.when(mine)(lambda part=part: settle_bytes(part, ring_recv.at[j, pair]))

    def forward_up(j):
        arrived(j, 0)
        pl.when(~top)(lambda: deep_up(j).start())

    def forward(j):
        for k in range(AHEAD + 1) if j == 0 else (j + AHEAD,):
            if k < PIECES:
                forward_up(k)
        arrived(j, 1)
        pl.when(~bottom)(lambda: deep_down(j).start())

    def settle_mix(levels, sink, start):
        share = v_diffusion
        keep, fall = 1.0 - 2.0 * share - sink, share + sink
        fresh = []
        for k in range(len(levels) - 2):
            upper, own, lower = levels[k : k + 3]
            upper_term = fall * upper
            lower_term = share * lower
            if start + k == 2:
                upper_term = jnp.where(top, share * own, upper_term)
            if start + k == 5:
                lower_term = jnp.where(bottom, share * own, lower_term)
            fresh.append(keep * own + upper_term + lower_term)
        return fresh

    def vertical(j, first, wide):
        for q in range(QUADS):
            spot = j * PART + 4 * q
            sink = sinks[j * QUADS + q]
            rows = []
            for r in range(4):
                levels = [column[first - 2 + k, spot + r] for k in range(wide + 4)]
                rows.append(settle_mix(settle_mix(levels, sink, first - 1), sink, first))
            for k in range(wide):
                for r in range(4):
                    mixed[first - 2 + k, spot + r] = rows[r][k]
        for level in range(first - 2, first - 2 + wide):
            pl.when(x != level)(lambda level=level: back(j, level, x).start())

    def upper_half(j):
        pl.when(~top)(lambda: deep_down(j).wait_recv())
        vertical(j, 2, 2)

    def lower_half(j):
        pl.when(~bottom)(lambda: deep_up(j).wait_recv())
        vertical(j, 4, 2)

    def follow(lead, lag):
        for j in range(lead):
            forward(j)
        for j in range(PIECES + lag):
            if j < PIECES:
                upper_half(j)
            if j >= lag:
                lower_half(j - lag)
            if lead + j < PIECES:
                forward(lead + j)

    corner = band < 2
    together = z > depth // 2
    start = top & corner
    next_corner = (z == 1) & corner
    apart = ~together & ~start & ~next_corner
    pl.when(together)(lambda: follow(4, 1))
    pl.when(apart)(lambda: follow(6, 2))
    pl.when(start)(lambda: follow(2, 0))
    pl.when(next_corner)(lambda: follow(PIECES, 0))

    for i in range(GROUP):
        settled[x, i] = mixed[x, i]
    settle_bytes(settled.at[pl.ds(0, 3)], back_recv)
    settle_bytes(moved.at[pl.ds(1, 3)], ring_send)
    settle_bytes(mixed.at[pl.ds(0, 3)], back_send)
    pl.when(~top)(lambda: settle_bytes(column.at[pl.ds(2, 2)], deep_send.at[1]))
    pl.when(~bottom)(lambda: settle_bytes(column.at[pl.ds(4, 2)], deep_send.at[0]))
    pl.when(~first_band)(lambda: settle_bytes(up_out, up_send))
    pl.when(~last_band)(lambda: settle_bytes(down_out, down_send))


def collide_kernel(settled, tables, out_hbm, cells_by_bin, out, sums, out_sem):
    parts = NB // SPAN

    def row(k, b):
        return jnp.broadcast_to(tables[k, pl.ds(b, 1)], (SUB, LANE))

    def store(p):
        part = pl.ds(p * SPAN, SPAN)
        return pltpu.make_async_copy(out.at[part], out_hbm.at[part], out_sem.at[p])

    def total(p, unused):
        b = p * SPAN
        cells = []
        for q in range(0, SPAN, 4):
            cells += swap_rows(*[settled[b + q + r] for r in range(4)])
        for i in range(SPAN):
            cells_by_bin[b + i] = cells[i]
        for k in range(3):
            terms = [row(k, b + i) * cells[i] for i in range(SPAN)]
            while len(terms) > 1:
                terms = [one + two for one, two in zip(terms[::2], terms[1::2])]
            sums[k, p] = terms[0]
        return unused

    lax.fori_loop(0, parts, total, 0, unroll=4)
    lower = jnp.zeros((SUB, LANE), jnp.float32)
    for p in range(parts):
        own = sums[0, p]
        sums[0, p] = lower
        lower = lower + own
    for k in (1, 2):
        higher = jnp.zeros((SUB, LANE), jnp.float32)
        for p in reversed(range(parts)):
            higher = higher + sums[k, p]
            sums[k, p] = higher

    def collide(p, unused):
        lower, higher, pieces = sums[0, p], sums[1, p], sums[2, p]
        for i in range(SPAN):
            b = p * SPAN + i
            cells = cells_by_bin[b]
            loss, gain = row(0, b), row(1, b)
            higher = higher - gain * cells
            pieces = pieces - row(2, b) * cells
            out[b] = cells * (row(3, b) + ALPHA * (gain * lower - loss * higher)) + pieces
            lower = lower + loss * cells
        store(p).start()
        return unused

    lax.fori_loop(0, parts, collide, 0, unroll=4)

    def finish(p, unused):
        store(p).wait()
        return unused

    lax.fori_loop(0, parts, finish, 0)


def local(depth, bands, conc, *rest):
    cells = conc.reshape(NB, 4, 2, LANE).transpose(0, 2, 1, 3).reshape(NB, SUB, LANE)
    vmem = pl.BlockSpec(memory_space=pltpu.VMEM)
    dma = pltpu.SemaphoreType.DMA
    tile = (SUB, LANE)

    def buffer(*shape):
        return pltpu.VMEM(shape + tile, jnp.float32)

    settled, tables = pl.pallas_call(
        functools.partial(step_kernel, depth, bands),
        out_shape=(
            jax.ShapeDtypeStruct((RING, GROUP) + tile, jnp.float32),
            jax.ShapeDtypeStruct((4, NB, LANE), jnp.float32),
        ),
        in_specs=[pl.BlockSpec(memory_space=pltpu.HBM)] * 9,
        out_specs=(vmem, vmem),
        scratch_shapes=[
            buffer(NB),
            pltpu.VMEM((1, 4, 2 * LANE), jnp.float32),
            pltpu.VMEM((1, 4, 2 * LANE), jnp.float32),
            pltpu.VMEM((4, 2 * LANE), jnp.int32),
            pltpu.VMEM((NB,), jnp.float32),
            pltpu.VMEM((NB,), jnp.int32),
            pltpu.SMEM((NCLS,), jnp.float32),
            pltpu.SMEM((NCLS,), jnp.float32),
            pltpu.SMEM((NCLS,), jnp.float32),
            buffer(MESSAGE),
            buffer(MESSAGE),
            buffer(MESSAGE),
            buffer(MESSAGE),
            buffer(RING, GROUP),
            buffer(8, GROUP),
            buffer(RING, GROUP),
            buffer(GROUP // 4),
            buffer(6, 5),
            dma((9,)),
            pltpu.SemaphoreType.REGULAR,
            pltpu.SemaphoreType.REGULAR,
            dma,
            dma((PIECES,)),
            dma,
            dma((PIECES,)),
            dma,
            dma((PIECES, 2)),
            dma((2,)),
            dma((PIECES, 2)),
            dma,
            dma,
        ],
        compiler_params=pltpu.CompilerParams(
            collective_id=0, has_side_effects=True, vmem_limit_bytes=20 << 20
        ),
    )(*[pltpu.with_memory_space_constraint(value, pltpu.HBM) for value in (cells, *rest)])
    result = pl.pallas_call(
        collide_kernel,
        out_shape=jax.ShapeDtypeStruct((NB,) + tile, jnp.float32),
        in_specs=[vmem, vmem],
        out_specs=pl.BlockSpec(memory_space=pl.ANY),
        scratch_shapes=[buffer(NB), buffer(NB), buffer(3, NB // SPAN), dma((NB // SPAN,))],
        compiler_params=pltpu.CompilerParams(vmem_limit_bytes=8 << 20),
    )(settled.reshape((NB,) + tile), tables)
    return result.reshape(NB, 2, 4, LANE).transpose(0, 2, 1, 3).reshape(conc.shape)


def solution(mesh):
    placed = (
        P("bins", None, "xy", None),
        P("bins", "xy", None),
        P("bins", "xy", None),
        P("xy", None),
        P(),
        P(),
        P(),
        P(),
        P(),
    )
    return jax.shard_map(
        functools.partial(local, mesh.shape["bins"] // RING, mesh.shape["xy"]),
        mesh=mesh,
        in_specs=placed,
        out_specs=P("bins", None, "xy", None),
        check_vma=False,
    )
```
